512 devices in a mesh: cells: 64 (over z, x), snaps: 8 (over y, core).
Axes of the slice: x: 4, y: 4, z: 16, core: 2. Of those that a mesh axis runs over, the one named last changes fastest.
Arguments:
- snapshots: float32 [262144, 2048], P('cells', 'snaps'), may hold values from -6 to 6
- sketch: float32 [2048, 32], P('snaps'), may hold values from -6 to 6
Outputs:
- basis: float32 [32, 262144], P(None, 'cells')
- coefficients: float32 [32, 2048], P(None, 'snaps')
The draws below stay inside these ranges and needn't reach their ends.
All inputs are finite; a program needn't handle non-finite values.
Results may differ from the reference program's by a relative error of at most 0.0003.
Values sent between devices are 32-bit elements; how exact they have to be, the bound alone decides.
A program may use at most 64 MiB of HBM per device.

```python
import math
import jax
import jax.numpy as jnp
from jax import lax

RANK = 32
CELLS = 262144
SNAPS = 2048


def shard_levels(rng, shape, shards, least, top_value):
    def one(axis_at, shards_of):
        heights = jax.random.uniform(jax.random.fold_in(jax.random.fold_in(rng, 6), axis_at), (shards_of,), jnp.float32, least / len(shards), top_value / len(shards))
        return jnp.repeat(jnp.exp(heights), shape[axis_at] // shards_of).reshape((-1,) + (1,) * (len(shape) - axis_at - 1))

    level = one(*shards[0])
    for cut in shards[1:]:
        level = level * one(*cut)
    return level


def centred(key, dims, deviation, most, split=(), kind=jnp.bfloat16):
    result = deviation * jax.random.normal(key, dims, jnp.float32)
    if split:
        result = result * shard_levels(key, dims, split, -0.22, 0.18)
    return jnp.clip(result, -most, most).astype(kind)


def setup_inputs(seed: int = 0) -> dict:
    streams_of = jax.random.split(jax.random.key(seed), 3)
    return {
        "snapshots": centred(streams_of[0], (CELLS, SNAPS), 1.0, 6.0, ((0, 64), (1, 8)), jnp.float32),
        "sketch": centred(streams_of[1], (SNAPS, RANK), 1.0, 6.0, ((0, 8),), jnp.float32),
    }


def reference(snapshots, sketch):
    sketched = jnp.einsum('sk,ms->km', sketch, snapshots, precision=lax.Precision.HIGHEST)
    factor_q, factor_r = jnp.linalg.qr(sketched.T)
    diagonal = jnp.diagonal(factor_r)
    sense = jnp.where(diagonal < 0, -1.0, 1.0).astype(factor_q.dtype)
    orth = (factor_q * sense[None, :]).T
    coefficients = jnp.dot(orth, snapshots, precision=lax.Precision.HIGHEST)
    basis = orth * math.sqrt(CELLS)
    return (basis, coefficients)
```

```python
import functools
import math

import jax
import jax.numpy as jnp
from jax import lax
from jax.experimental import pallas as pl
from jax.experimental.pallas import tpu as pltpu
from jax.sharding import PartitionSpec as P

MESH = pl.DeviceIdType.MESH
NX = 4
F32 = jnp.float32
BF16 = jnp.bfloat16
ROWS = 32


def two_sum(a, b):
    s = a + b
    t = s - a
    return s, (a - (s - t)) + (b - t)


def quick_two_sum(a, b):
    s = a + b
    return s, b - (s - a)


def halves(a):
    c = a * 4097.0
    high = c - (c - a)
    return high, a - high


def two_prod(a, ah, al, b, bh, bl):
    p = a * b
    return p, ((ah * bh - p) + ah * bl + al * bh) + al * bl


def dd_add(ah, al, bh, bl):
    s, e = two_sum(ah, bh)
    return quick_two_sum(s, e + (al + bl))


def thirds(a):
    h = a.astype(BF16)
    rest = a - h.astype(F32)
    m = rest.astype(BF16)
    low = (rest - m.astype(F32)).astype(BF16)
    return h, m, low


def dot(a, b, transposed=False):
    dims = (((1,), (1 if transposed else 0,)), ((), ()))
    return lax.dot_general(a, b, dims, preferred_element_type=F32)


def six(lhs, h, m, low, transposed):
    n = ROWS
    dh = dot(lhs, h, transposed)
    dm = dot(lhs[: 2 * n], m, transposed)
    dl = dot(lhs[:n], low, transposed)
    small = (dh[2 * n :] + dm[n:]) + dl
    return dh[:n] + ((dh[n : 2 * n] + dm[:n]) + small)


def sum_pairs(pairs):
    while len(pairs) > 1:
        pairs = [
            dd_add(*pairs[i], *pairs[i + 1]) if i + 1 < len(pairs) else pairs[i]
            for i in range(0, len(pairs), 2)
        ]
    return pairs[0]


def power_above(x):
    p = jnp.full(x.shape, 2.0**-63, F32)
    inverse = jnp.full(x.shape, 2.0**63, F32)
    for step in (64, 32, 16, 8, 4, 2, 1):
        larger = x >= p * (2.0**step)
        p = jnp.where(larger, p * (2.0**step), p)
        inverse = jnp.where(larger, inverse * (2.0**-step), inverse)
    return p * 2.0, inverse * 0.5


def eliminate(gh, gl):
    gh, gl = list(gh), list(gl)
    tiles = len(gh)
    sub = lax.broadcasted_iota(jnp.int32, (8, 128), 0)
    lane = lax.broadcasted_iota(jnp.int32, (8, 128), 1)
    for k in range(8 * tiles - 1):
        ib, kr = divmod(k, 8)
        rh = jnp.broadcast_to(gh[ib][kr : kr + 1, :], (8, 128))
        rl = jnp.broadcast_to(gl[ib][kr : kr + 1, :], (8, 128))
        ph = jnp.broadcast_to(rh[:, k : k + 1], (8, 128))
        plo = jnp.broadcast_to(rl[:, k : k + 1], (8, 128))
        r = 1.0 / ph
        pa, pb = halves(ph)
        q1 = rh * r
        qa, qb = halves(q1)
        t, te = two_prod(q1, qa, qb, ph, pa, pb)
        rest = (rh - t) - te + (rl - q1 * plo)
        uh, ul = quick_two_sum(q1, rest * r)
        ua, ub = halves(uh)
        for t in range(ib if kr < 7 else ib + 1, tiles):
            ch = jnp.broadcast_to(gh[t][:, k : k + 1], (8, 128))
            cl = jnp.broadcast_to(gl[t][:, k : k + 1], (8, 128))
            if t == ib:
                ch = jnp.where(sub > kr, ch, 0.0)
                cl = jnp.where(sub > kr, cl, 0.0)
            ca, cb = halves(ch)
            p, pe = two_prod(ch, ca, cb, uh, ua, ub)
            pe = pe + (ch * ul + cl * uh)
            s, e = two_sum(gh[t], -p)
            gh[t], gl[t] = quick_two_sum(s, e + (gl[t] - pe))
    out = []
    for t in range(tiles):
        at = lane == sub + 8 * t
        d = jnp.sum(jnp.where(at, gh[t], 0.0), axis=1, keepdims=True)
        y = lax.rsqrt(d)
        y = y * (1.5 - 0.5 * d * y * y)
        out.append((gh[t] + gl[t]) * y)
    return out


def kernel(
    nz, ch, total_cells,
    a_ref, w_ref, basis_ref, coef_ref,
    a_buf, a_h, a_m, a_l,
    send_a, got_a, rs_a, rs_b, rs_c, rs_d, s_all, s_cat,
    x_bf, p_ref, sig, gx, gz, ga, gt,
    wp, wx, wz, wa,
    load_sem, s_a, r_a, s_b, r_b, s_y, r_y, s_f, r_f, s_p, r_p, s_m, r_m,
):
    cells = lax.axis_index("cells")
    snaps = lax.axis_index("snaps")
    z, x = cells // NX, cells % NX
    y, core = snaps // 2, snaps % 2
    n = ROWS
    up, down, far = (y + 1) % 4, (y + 3) % 4, (y + 2) % 4
    mate = (cells, y * 2 + (1 - core))
    above = (cells, up * 2 + core)
    below = (cells, down * 2 + core)
    snap_peers = [(cells, (snaps + d) % 8) for d in (4, 5, 3, 2, 6, 1, 7)]
    x_peers = [(z * NX + (x + d) % NX, snaps) for d in range(1, NX)]
    z_steps = sorted(range(1, nz), key=lambda d: -min(d, nz - d))
    z_peers = [(((z + d) % nz) * NX + x, snaps) for d in z_steps]

    def remote(src, dst, ss, rs, to):
        return pltpu.make_async_remote_copy(
            src_ref=src, dst_ref=dst, send_sem=ss, recv_sem=rs,
            device_id=to, device_id_type=MESH,
        )

    barrier = pltpu.get_barrier_semaphore()
    everyone = z_peers + x_peers + snap_peers
    for peer in everyone:
        pl.semaphore_signal(barrier, inc=1, device_id=peer, device_id_type=MESH)

    offsets = (far, up, down, y)
    order = [(1 - core, o) for o in offsets] + [(core, o) for o in offsets]
    chunk_of = [c * 4 + o for c, o in order]
    loads = []
    for i, q in enumerate(chunk_of):
        start = pl.multiple_of(q * ch, ch)
        loads.append(
            pltpu.make_async_copy(a_ref.at[pl.ds(start, ch), :], a_buf.at[i], load_sem.at[i])
        )
        loads[-1].start()

    w_h, w_m, w_l = thirds(w_ref[...])
    w_cat = jnp.concatenate([w_h, w_m, w_l], axis=0)

    def sketch_chunk(i):
        loads[i].wait()
        h, m, low = thirds(a_buf[i])
        a_h[i], a_m[i], a_l[i] = h, m, low
        return six(w_cat, h, m, low, True)

    swaps = []
    for i in range(4):
        send_a[i] = sketch_chunk(i)
        if i == 0:
            pl.semaphore_wait(barrier, len(everyone))
        swaps.append(remote(send_a.at[i], got_a.at[i], s_a.at[i], r_a.at[i], mate))
        swaps[-1].start()

    far_part = sketch_chunk(4)
    swaps[0].wait_recv()
    rs_a[...] = far_part + got_a[0]
    b_up = remote(rs_a.at[0:16], rs_b.at[0], s_b.at[0], r_b.at[0], above)
    b_up.start()
    b_down = remote(rs_a.at[16:32], rs_b.at[1], s_b.at[1], r_b.at[1], below)
    b_down.start()
    up_part = sketch_chunk(5)
    swaps[1].wait_recv()
    up_part = up_part + got_a[1]
    rs_c[0, 16:32] = up_part[16:32]
    down_part = sketch_chunk(6)
    swaps[2].wait_recv()
    down_part = down_part + got_a[2]
    rs_c[1, 0:16] = down_part[0:16]
    b_up.wait_recv()
    rs_c[0, 0:16] = up_part[0:16] + rs_b[0]
    c_up = remote(rs_c.at[0], rs_d.at[0], s_b.at[2], r_b.at[2], above)
    c_up.start()
    b_down.wait_recv()
    rs_c[1, 16:32] = down_part[16:32] + rs_b[1]
    c_down = remote(rs_c.at[1], rs_d.at[1], s_b.at[3], r_b.at[3], below)
    c_down.start()
    own_part = sketch_chunk(7)
    swaps[3].wait_recv()
    own_part = own_part + got_a[3]
    c_up.wait_recv()
    own_part = own_part + rs_d[0]
    c_down.wait_recv()
    own = core * 4 + y
    s_all[own] = own_part + rs_d[1]

    g_up = remote(s_all.at[own], s_all.at[own], s_y.at[0], r_y.at[0], above)
    g_up.start()
    g_down = remote(s_all.at[own], s_all.at[own], s_y.at[1], r_y.at[1], below)
    g_down.start()

    def pass_on(slot, sem):
        copy = remote(s_all.at[slot], s_all.at[slot], s_p.at[sem], r_p.at[sem], mate)
        copy.start()
        return copy

    passes = [pass_on(own, 0)]

    def projected(i, slot):
        s_h, s_m, s_l = thirds(s_all[slot])
        s_cat[slot, 0:n] = s_h
        s_cat[slot, n : 2 * n] = s_m
        s_cat[slot, 2 * n : 3 * n] = s_l
        s_cat[slot, 3 * n : 4 * n] = s_h
        s_cat[slot, 4 * n : 5 * n] = s_m
        s_cat[slot, 5 * n : 6 * n] = s_h
        lhs = jnp.concatenate([s_h, s_m, s_l], axis=0)
        return six(lhs, a_h[i], a_m[i], a_l[i], False)

    w_sum = projected(7, own)
    passes[0].wait_recv()
    w_sum += projected(3, (1 - core) * 4 + y)
    slot_down, slot_up, slot_far = core * 4 + down, core * 4 + up, core * 4 + far
    arrived = remote(s_all.at[slot_down], s_all.at[slot_down], s_y.at[0], r_y.at[0], above)
    arrived.wait_recv()
    f_up = remote(
        s_all.at[slot_down, 0:16], s_all.at[slot_down, 0:16], s_f.at[0], r_f.at[0], above
    )
    f_up.start()
    passes.append(pass_on(slot_down, 1))
    arrived = remote(s_all.at[slot_up], s_all.at[slot_up], s_y.at[1], r_y.at[1], below)
    arrived.wait_recv()
    f_down = remote(
        s_all.at[slot_up, 16:32], s_all.at[slot_up, 16:32], s_f.at[1], r_f.at[1], below
    )
    f_down.start()
    passes.append(pass_on(slot_up, 2))
    w_sum += projected(6, slot_down)
    w_sum += projected(5, slot_up)
    passes[1].wait_recv()
    w_sum += projected(2, (1 - core) * 4 + down)
    passes[2].wait_recv()
    w_sum += projected(1, (1 - core) * 4 + up)
    f_up.wait_recv()
    f_down.wait_recv()
    passes.append(pass_on(slot_far, 3))
    w_sum += projected(4, slot_far)
    passes[3].wait_recv()
    w_sum += projected(0, (1 - core) * 4 + far)

    share = n // NX
    for i in range(NX):
        wp[i] = w_sum[i * share : (i + 1) * share]
    wx[x] = wp[x]
    for peer in x_peers:
        remote(wp.at[peer[0] % NX], wx.at[x], s_m.at[0], r_m.at[0], peer).start()

    top = jnp.max(jnp.abs(s_all[0]), axis=1, keepdims=True)
    for q in range(1, 8):
        top = jnp.maximum(top, jnp.max(jnp.abs(s_all[q]), axis=1, keepdims=True))
    scale, inverse = power_above(jnp.broadcast_to(top, (n, 128)))
    sig[...] = scale
    up_scale = inverse[:, 0:1] * 64.0
    p_sum = None
    for q in range(8):
        v = s_all[q] * up_scale
        parts = []
        for a in range(4):
            whole = jnp.round(v)
            parts.append(whole.astype(BF16))
            v = (v - whole) * 128.0
        x_bf[...] = jnp.concatenate(parts, axis=0)
        term = dot(x_bf[...], x_bf[...], True)
        p_sum = term if p_sum is None else p_sum + term
    p_ref[...] = p_sum
    part = p_ref[pl.ds(snaps, 16, stride=8), :]
    lane = lax.broadcasted_iota(jnp.int32, (4, 128), 1)
    group = lane // n
    lane_weight = jnp.where(
        group == 0, 2.0**-12, jnp.where(group == 1, 2.0**-19, jnp.where(group == 2, 2.0**-26, 2.0**-33))
    )
    gh = part[0:4] * lane_weight
    gl = jnp.zeros((4, 128), F32)
    for a in range(1, 4):
        gh, gl = dd_add(gh, gl, part[4 * a : 4 * a + 4] * (lane_weight * 2.0 ** (-7 * a)), 0.0)
    for turn in (64, 32):
        gh, gl = dd_add(gh, gl, pltpu.roll(gh, turn, 1), pltpu.roll(gl, turn, 1))
    row_scale = sig[pl.ds(snaps, 4, stride=8), :]
    wide = lax.broadcasted_iota(jnp.int32, (n, 128), 1)
    tall = lax.broadcasted_iota(jnp.int32, (n, 128), 0)
    column_scale = jnp.sum(jnp.where(wide % n == tall, scale, 0.0), axis=0, keepdims=True)
    both = row_scale * column_scale
    pick = lax.broadcasted_iota(jnp.int32, (4, 128), 0) == group
    gx[x, 0] = jnp.sum(jnp.where(pick, gh * both, 0.0), axis=0, keepdims=True)
    gx[x, 1] = jnp.sum(jnp.where(pick, gl * both, 0.0), axis=0, keepdims=True)

    def slots(buf, count):
        return buf.at[pl.ds(0, count)]

    for peer in x_peers:
        remote(gx.at[x], gx.at[x], s_m.at[1], r_m.at[1], peer).start()
    few = remote(slots(gx, NX - 1), slots(gx, NX - 1), s_m.at[1], r_m.at[1], mate)
    few.wait_recv()
    hi, lo = sum_pairs([(gx[i, 0], gx[i, 1]) for i in range(NX)])
    gz[z, 0], gz[z, 1] = hi, lo
    for peer in z_peers:
        remote(gz.at[z], gz.at[z], s_m.at[2], r_m.at[2], peer).start()

    w_few = remote(slots(wx, NX - 1), slots(wx, NX - 1), s_m.at[0], r_m.at[0], mate)
    w_few.wait_recv()
    row_sum = wx[0]
    for i in range(1, NX):
        row_sum = row_sum + wx[i]
    wz[z] = row_sum
    for peer in z_peers:
        remote(wz.at[z], wz.at[z], s_m.at[3], r_m.at[3], peer).start()

    g_many = remote(slots(gz, nz - 1), slots(gz, nz - 1), s_m.at[2], r_m.at[2], mate)
    g_many.wait_recv()
    hi, lo = sum_pairs([(gz[i, 0], gz[i, 1]) for i in range(nz)])
    ga[snaps, 0], ga[snaps, 1] = hi, lo
    for peer in snap_peers:
        remote(ga.at[snaps], ga.at[snaps], s_m.at[4], r_m.at[4], peer).start()
    g_seven = remote(slots(ga, 7), slots(ga, 7), s_m.at[4], r_m.at[4], mate)
    g_seven.wait_recv()

    for r in range(8):
        gt[0, r : r + 1, :] = ga[r, 0]
        gt[1, r : r + 1, :] = ga[r, 1]
    lane8 = lax.broadcasted_iota(jnp.int32, (8, 128), 1)
    sub8 = lax.broadcasted_iota(jnp.int32, (8, 128), 0)
    tiles_h, tiles_l = [], []
    for i in range(4):
        eye = jnp.where(lane8 - n == sub8 + 8 * i, 1.0, 0.0)
        turned_h = gt[0] if i == 0 else pltpu.roll(gt[0], 128 - n * i, 1)
        turned_l = gt[1] if i == 0 else pltpu.roll(gt[1], 128 - n * i, 1)
        tiles_h.append(jnp.where(lane8 < n, turned_h, eye))
        tiles_l.append(jnp.where(lane8 < n, turned_l, 0.0))
    factor = jnp.concatenate(eliminate(tiles_h, tiles_l), axis=0)
    f_h, f_m, f_l = thirds(factor)
    f_h, f_m, f_l = f_h.astype(F32), f_m.astype(F32), f_l.astype(F32)
    which = wide // n
    first = jnp.where(
        which == 0, pltpu.roll(f_h, 96, 1),
        jnp.where(which == 1, f_h, jnp.where(which == 2, pltpu.roll(f_h, 32, 1), pltpu.roll(f_m, 64, 1))),
    )
    second = jnp.where(which == 0, pltpu.roll(f_m, 96, 1), f_l)
    inv_cat = jnp.concatenate([first, second[:, : 2 * n]], axis=1).astype(BF16)
    root = math.sqrt(total_cells)
    for q in range(8):
        basis_ref[:, q * ch : (q + 1) * ch] = dot(inv_cat, s_cat[q]) * root

    w_many = remote(slots(wz, nz - 1), slots(wz, nz - 1), s_m.at[3], r_m.at[3], mate)
    w_many.wait_recv()
    rows = [wz[i] for i in range(nz)]
    while len(rows) > 1:
        rows = [rows[i] + rows[i + 1] for i in range(0, len(rows), 2)]
    wa[x] = rows[0]
    for peer in x_peers:
        remote(wa.at[x], wa.at[x], s_m.at[5], r_m.at[5], peer).start()
    wa_few = remote(slots(wa, NX - 1), slots(wa, NX - 1), s_m.at[5], r_m.at[5], mate)
    wa_few.wait_recv()
    w_total = jnp.concatenate([wa[i] for i in range(NX)], axis=0)
    t_h, t_m, t_l = thirds(w_total)
    w_parts = jnp.concatenate([t_h, t_m, t_l, t_h, t_m, t_h], axis=0)
    coef_ref[...] = dot(inv_cat, w_parts)

    for copy in swaps + [b_up, b_down, c_up, c_down, g_up, g_down, f_up, f_down] + passes:
        copy.wait_send()
    for copy in (w_few, few, g_many, w_many, g_seven, wa_few):
        copy.wait_send()


def shards(snapshots, sketch):
    cells, snaps = snapshots.shape
    n = sketch.shape[1]
    nz = lax.axis_size("cells") // NX
    ch = cells // 8
    total = cells * lax.axis_size("cells")
    dma = pltpu.SemaphoreType.DMA
    vm = pltpu.VMEM
    return pl.pallas_call(
        functools.partial(kernel, nz, ch, total),
        out_shape=(
            jax.ShapeDtypeStruct((n, cells), F32),
            jax.ShapeDtypeStruct((n, snaps), F32),
        ),
        in_specs=[
            pl.BlockSpec(memory_space=pl.ANY),
            pl.BlockSpec(memory_space=pltpu.VMEM),
        ],
        out_specs=(
            pl.BlockSpec(memory_space=pltpu.VMEM),
            pl.BlockSpec(memory_space=pltpu.VMEM),
        ),
        scratch_shapes=[
            vm((8, ch, snaps), F32),
            vm((8, ch, snaps), BF16), vm((8, ch, snaps), BF16), vm((8, ch, snaps), BF16),
            vm((4, n, ch), F32), vm((4, n, ch), F32),
            vm((n, ch), F32), vm((2, n // 2, ch), F32),
            vm((2, n, ch), F32), vm((2, n, ch), F32),
            vm((8, n, ch), F32), vm((8, 6 * n, ch), BF16),
            vm((4 * n, ch), BF16), vm((128, 128), F32), vm((n, 128), F32),
            vm((NX, 2, 1, 128), F32), vm((nz, 2, 1, 128), F32),
            vm((8, 2, 1, 128), F32), vm((2, 8, 128), F32),
            vm((NX, n // NX, snaps), F32), vm((NX, n // NX, snaps), F32),
            vm((nz, n // NX, snaps), F32), vm((NX, n // NX, snaps), F32),
            dma((8,)), dma((4,)), dma((4,)), dma((4,)), dma((4,)),
            dma((2,)), dma((2,)), dma((2,)), dma((2,)), dma((4,)), dma((4,)),
            dma((6,)), dma((6,)),
        ],
        compiler_params=pltpu.CompilerParams(collective_id=0, has_side_effects=True),
    )(snapshots, jnp.transpose(sketch))


def solution(mesh):
    return jax.shard_map(
        shards,
        mesh=mesh,
        in_specs=(P("cells", "snaps"), P("snaps", None)),
        out_specs=(P(None, "cells"), P(None, "snaps")),
        check_vma=False,
    )
```

```python
import functools
import math

import jax
import jax.numpy as jnp
from jax import lax
from jax.experimental import pallas as pl
from jax.experimental.pallas import tpu as pltpu
from jax.sharding import PartitionSpec as P

MESH = pl.DeviceIdType.MESH
NX = 4
F32 = jnp.float32
BF16 = jnp.bfloat16
ROWS = 32


def two_sum(a, b):
    s = a + b
    t = s - a
    return s, (a - (s - t)) + (b - t)


def quick_two_sum(a, b):
    s = a + b
    return s, b - (s - a)


def halves(a):
    c = a * 4097.0
    high = c - (c - a)
    return high, a - high


def two_prod(a, ah, al, b, bh, bl):
    p = a * b
    return p, ((ah * bh - p) + ah * bl + al * bh) + al * bl


def dd_add(ah, al, bh, bl):
    s, e = two_sum(ah, bh)
    return quick_two_sum(s, e + (al + bl))


def thirds(a):
    h = a.astype(BF16)
    rest = a - h.astype(F32)
    m = rest.astype(BF16)
    low = (rest - m.astype(F32)).astype(BF16)
    return h, m, low


def dot(a, b, transposed=False):
    dims = (((1,), (1 if transposed else 0,)), ((), ()))
    return lax.dot_general(a, b, dims, preferred_element_type=F32)


def six(lhs, h, m, low, transposed):
    n = ROWS
    dh = dot(lhs, h, transposed)
    dm = dot(lhs[: 2 * n], m, transposed)
    dl = dot(lhs[:n], low, transposed)
    small = (dh[2 * n :] + dm[n:]) + dl
    return dh[:n] + ((dh[n : 2 * n] + dm[:n]) + small)


def sum_pairs(pairs):
    while len(pairs) > 1:
        pairs = [
            dd_add(*pairs[i], *pairs[i + 1]) if i + 1 < len(pairs) else pairs[i]
            for i in range(0, len(pairs), 2)
        ]
    return pairs[0]


def power_above(x):
    p = jnp.full(x.shape, 2.0**-63, F32)
    inverse = jnp.full(x.shape, 2.0**63, F32)
    for step in (64, 32, 16, 8, 4, 2, 1):
        larger = x >= p * (2.0**step)
        p = jnp.where(larger, p * (2.0**step), p)
        inverse = jnp.where(larger, inverse * (2.0**-step), inverse)
    return p * 2.0, inverse * 0.5


def eliminate(gh, gl):
    gh, gl = list(gh), list(gl)
    tiles = len(gh)
    sub = lax.broadcasted_iota(jnp.int32, (8, 128), 0)
    lane = lax.broadcasted_iota(jnp.int32, (8, 128), 1)
    for k in range(8 * tiles - 1):
        ib, kr = divmod(k, 8)
        rh = jnp.broadcast_to(gh[ib][kr : kr + 1, :], (8, 128))
        rl = jnp.broadcast_to(gl[ib][kr : kr + 1, :], (8, 128))
        ph = jnp.broadcast_to(rh[:, k : k + 1], (8, 128))
        plo = jnp.broadcast_to(rl[:, k : k + 1], (8, 128))
        r = 1.0 / ph
        pa, pb = halves(ph)
        q1 = rh * r
        qa, qb = halves(q1)
        t, te = two_prod(q1, qa, qb, ph, pa, pb)
        rest = (rh - t) - te + (rl - q1 * plo)
        uh, ul = quick_two_sum(q1, rest * r)
        ua, ub = halves(uh)
        for t in range(ib if kr < 7 else ib + 1, tiles):
            ch = jnp.broadcast_to(gh[t][:, k : k + 1], (8, 128))
            cl = jnp.broadcast_to(gl[t][:, k : k + 1], (8, 128))
            if t == ib:
                ch = jnp.where(sub > kr, ch, 0.0)
                cl = jnp.where(sub > kr, cl, 0.0)
            ca, cb = halves(ch)
            p, pe = two_prod(ch, ca, cb, uh, ua, ub)
            pe = pe + (ch * ul + cl * uh)
            s, e = two_sum(gh[t], -p)
            gh[t], gl[t] = quick_two_sum(s, e + (gl[t] - pe))
    out = []
    for t in range(tiles):
        at = lane == sub + 8 * t
        d = jnp.sum(jnp.where(at, gh[t], 0.0), axis=1, keepdims=True)
        y = lax.rsqrt(d)
        y = y * (1.5 - 0.5 * d * y * y)
        out.append((gh[t] + gl[t]) * y)
    return out


def packed_gram(rows):
    n = ROWS
    top = jnp.max(jnp.abs(rows), axis=1, keepdims=True)
    scale, inverse = power_above(jnp.broadcast_to(top, (n, 128)))
    v = rows * (inverse[:, 0:1] * 64.0)
    parts = []
    for a in range(4):
        whole = jnp.round(v)
        parts.append(whole.astype(BF16))
        v = (v - whole) * 128.0
    slices = jnp.concatenate(parts, axis=0)
    products = dot(slices, slices, True)
    wide = lax.broadcasted_iota(jnp.int32, (n, 128), 1)
    tall = lax.broadcasted_iota(jnp.int32, (n, 128), 0)
    group = wide // n
    weight = jnp.where(
        group == 0, 2.0**-12,
        jnp.where(group == 1, 2.0**-19, jnp.where(group == 2, 2.0**-26, 2.0**-33)),
    )
    gh, gl = two_sum(products[0:n] * weight, products[n : 2 * n] * (weight * 2.0**-7))
    for a in (2, 3):
        gh, gl = dd_add(gh, gl, products[a * n : (a + 1) * n] * (weight * 2.0 ** (-7 * a)), 0.0)
    for turn in (64, 32):
        gh, gl = dd_add(gh, gl, pltpu.roll(gh, turn, 1), pltpu.roll(gl, turn, 1))
    column_scale = jnp.sum(jnp.where(wide - n * group == tall, scale, 0.0), axis=0, keepdims=True)
    both = scale * column_scale
    gh, gl = gh * both, gl * both
    lanes = lax.broadcasted_iota(jnp.int32, (8, 128), 1) // n

    def pack(g):
        out = g[0:8]
        for i in range(1, 4):
            out = jnp.where(lanes == i, g[8 * i : 8 * i + 8], out)
        return out

    return pack(gh), pack(gl)


def kernel(
    nz, ch, total_cells,
    a_ref, w_ref, basis_ref, coef_ref,
    a_buf, a_h, a_m, a_l,
    send_a, got_a, rs_a, rs_b, rs_c, rs_d, s_all, s_cat,
    go, gs, gx, gz, ga, gt,
    wp, wx, wz, wa, out_b, out_c,
    load_sem, s_a, r_a, s_b, r_b, s_c, r_c, s_y, r_y, s_f, r_f, s_p, r_p, s_m, r_m,
    out_sem, know_sem,
):
    cells = lax.axis_index("cells")
    snaps = lax.axis_index("snaps")
    n = ROWS
    ng, nu = 2 * NX, nz // 2
    z, x = lax.div(cells, NX), lax.rem(cells, NX)
    u, odd = lax.div(z, 2), lax.rem(z, 2)
    y, core = lax.div(snaps, 2), lax.rem(snaps, 2)
    g = 2 * x + odd
    up, down, far = lax.rem(y + 1, 4), lax.rem(y + 3, 4), lax.rem(y + 2, 4)
    mate = (cells, 2 * y + 1 - core)
    above = (cells, 2 * up + core)
    below = (cells, 2 * down + core)
    snap_of = [lax.rem(snaps + d, 8) for d in (4, 5, 3, 2, 6, 1, 7)]
    snap_peers = [(cells, s) for s in snap_of]
    g_of = [lax.rem(g + d, ng) for d in range(1, ng)]
    g_peers = [((2 * u + lax.rem(o, 2)) * NX + lax.div(o, 2), snaps) for o in g_of]

    def at_u(d):
        return ((2 * lax.rem(u + d, nu) + odd) * NX + x, snaps)

    u_peers = [at_u(d) for d in sorted(range(1, nu), key=lambda d: -min(d, nu - d))]

    def remote(src, dst, ss, rs, to):
        return pltpu.make_async_remote_copy(
            src_ref=src, dst_ref=dst, send_sem=ss, recv_sem=rs,
            device_id=to, device_id_type=MESH,
        )

    def signal(sem, to):
        pl.semaphore_signal(sem, inc=1, device_id=to, device_id_type=MESH)

    chunk_of = []
    for o in (far, up, down, y):
        chunk_of += [(1 - core) * 4 + o, core * 4 + o]
    loads = []
    for i, q in enumerate(chunk_of):
        start = pl.multiple_of(q * ch, ch)
        loads.append(
            pltpu.make_async_copy(a_ref.at[pl.ds(start, ch), :], a_buf.at[i], load_sem.at[i])
        )
        loads[-1].start()

    barrier = pltpu.get_barrier_semaphore()
    near = [at_u(1), at_u(nu - 1)] + g_peers + snap_peers
    for peer in near:
        signal(barrier, peer)

    w_h, w_m, w_l = thirds(w_ref[...])
    w_cat = jnp.concatenate([w_h, w_m, w_l], axis=0)

    def sketch_chunk(i):
        loads[i].wait()
        h, m, low = thirds(a_buf[i])
        a_h[i], a_m[i], a_l[i] = h, m, low
        return six(w_cat, h, m, low, True)

    swaps = []

    def swap(j):
        send_a[j] = sketch_chunk(2 * j)
        if j == 0:
            pl.semaphore_wait(barrier, len(near))
        swaps.append(remote(send_a.at[j], got_a.at[j], s_a.at[j], r_a.at[j], mate))
        swaps[-1].start()

    known = [1]

    def learn(part):
        while known[0] < nu // 2:
            d = known[0]
            sem = know_sem.at[d.bit_length() - 1]
            if part == 0:
                signal(sem, at_u(d))
                signal(sem, at_u(nu - d))
                return
            pl.semaphore_wait(sem, 2)
            known[0] = 2 * d
            return

    swap(0)
    learn(0)
    far_part = sketch_chunk(1)
    swap(1)
    up_part = sketch_chunk(3)
    swap(2)
    swaps[0].wait_recv()
    rs_a[...] = far_part + got_a[0]
    b_up = remote(rs_a.at[0:16], rs_b.at[0], s_b.at[0], r_b.at[0], above)
    b_up.start()
    b_down = remote(rs_a.at[16:32], rs_b.at[1], s_b.at[1], r_b.at[1], below)
    b_down.start()
    learn(1)
    learn(0)
    down_part = sketch_chunk(5)
    swaps[1].wait_recv()
    up_part = up_part + got_a[1]
    rs_c[0, 16:32] = up_part[16:32]
    c_up = [remote(rs_c.at[0, 16:32], rs_d.at[0, 16:32], s_c.at[0], r_c.at[0], above)]
    c_up[0].start()
    swap(3)
    swaps[2].wait_recv()
    down_part = down_part + got_a[2]
    rs_c[1, 0:16] = down_part[0:16]
    c_down = [remote(rs_c.at[1, 0:16], rs_d.at[1, 0:16], s_c.at[1], r_c.at[1], below)]
    c_down[0].start()
    own_part = sketch_chunk(7)
    b_up.wait_recv()
    rs_c[0, 0:16] = up_part[0:16] + rs_b[0]
    c_up.append(remote(rs_c.at[0, 0:16], rs_d.at[0, 0:16], s_c.at[2], r_c.at[2], above))
    c_up[1].start()
    b_down.wait_recv()
    rs_c[1, 16:32] = down_part[16:32] + rs_b[1]
    c_down.append(remote(rs_c.at[1, 16:32], rs_d.at[1, 16:32], s_c.at[3], r_c.at[3], below))
    c_down[1].start()
    swaps[3].wait_recv()
    own_part = own_part + got_a[3]
    learn(1)
    for copy in c_up + c_down:
        copy.wait_recv()
    own = core * 4 + y
    own_rows = own_part + rs_d[0] + rs_d[1]
    s_all[own] = own_rows

    first, second = pl.ds(0, 16), pl.ds(16, 16)

    def along(slot, rows, sem, to, s, r):
        piece = s_all.at[slot, rows]
        return remote(piece, piece, s.at[sem], r.at[sem], to)

    gathers = [
        along(own, first, 0, above, s_y, r_y),
        along(own, second, 1, below, s_y, r_y),
        along(own, second, 2, above, s_y, r_y),
        along(own, first, 3, below, s_y, r_y),
    ]
    for copy in gathers:
        copy.start()

    passes = []

    def pass_on(slot):
        sem = len(passes)
        copy = remote(s_all.at[slot], s_all.at[slot], s_p.at[sem], r_p.at[sem], mate)
        copy.start()
        passes.append(copy)

    pass_on(own)

    gram_h, gram_l = packed_gram(own_rows)
    for r in range(8):
        go[r, 0] = gram_h[r : r + 1]
        go[r, 1] = gram_l[r : r + 1]
    gs[snaps] = go[snaps]
    for s, peer in zip(snap_of, snap_peers):
        remote(go.at[s], gs.at[snaps], s_m.at[0], r_m.at[0], peer).start()

    def whole(buf, count, sem):
        piece = buf.at[pl.ds(0, count)]
        return remote(piece, piece, s_m.at[sem], r_m.at[sem], mate)

    def pair_sum(buf, count):
        return sum_pairs([(buf[i, 0], buf[i, 1]) for i in range(count)])

    def row_sum(buf, count):
        rows = [buf[i] for i in range(count)]
        while len(rows) > 1:
            rows = [rows[i] + rows[i + 1] for i in range(0, len(rows), 2)]
        return rows[0]

    def projected(i, slot):
        s_h, s_m, s_l = thirds(s_all[slot])
        s_cat[slot, 0:n] = s_h
        s_cat[slot, n : 2 * n] = s_m
        s_cat[slot, 2 * n : 3 * n] = s_l
        s_cat[slot, 3 * n : 4 * n] = s_h
        s_cat[slot, 4 * n : 5 * n] = s_m
        s_cat[slot, 5 * n : 6 * n] = s_h
        lhs = jnp.concatenate([s_h, s_m, s_l], axis=0)
        return six(lhs, a_h[i], a_m[i], a_l[i], False)

    theirs = (1 - core) * 4
    slot_down, slot_up, slot_far = core * 4 + down, core * 4 + up, core * 4 + far
    w_sum = projected(7, own)
    passes[0].wait_recv()
    w_sum += projected(6, theirs + y)
    along(slot_down, first, 0, above, s_y, r_y).wait_recv()
    f_up = along(slot_down, first, 0, above, s_f, r_f)
    f_up.start()
    along(slot_up, second, 1, below, s_y, r_y).wait_recv()
    f_down = along(slot_up, second, 1, below, s_f, r_f)
    f_down.start()
    along(slot_down, second, 2, above, s_y, r_y).wait_recv()
    pass_on(slot_down)
    along(slot_up, first, 3, below, s_y, r_y).wait_recv()
    pass_on(slot_up)

    gs_done = whole(gs, 7, 0)
    gs_done.wait_recv()
    hi, lo = pair_sum(gs, 8)
    gx[g, 0], gx[g, 1] = hi, lo
    for peer in g_peers:
        remote(gx.at[g], gx.at[g], s_m.at[1], r_m.at[1], peer).start()

    w_sum += projected(5, slot_down)
    w_sum += projected(3, slot_up)
    f_up.wait_recv()
    f_down.wait_recv()
    pass_on(slot_far)
    passes[1].wait_recv()
    w_sum += projected(4, theirs + down)
    passes[2].wait_recv()
    w_sum += projected(2, theirs + up)
    w_sum += projected(1, slot_far)
    passes[3].wait_recv()
    w_sum += projected(0, theirs + far)

    share = n // ng
    for i in range(ng):
        wp[i] = w_sum[i * share : (i + 1) * share]
    wx[g] = wp[g]
    for o, peer in zip(g_of, g_peers):
        remote(wp.at[o], wx.at[g], s_m.at[2], r_m.at[2], peer).start()

    gx_done = whole(gx, ng - 1, 1)
    gx_done.wait_recv()
    hi, lo = pair_sum(gx, ng)
    gz[u, 0], gz[u, 1] = hi, lo
    for peer in u_peers:
        remote(gz.at[u], gz.at[u], s_m.at[3], r_m.at[3], peer).start()

    wx_done = whole(wx, ng - 1, 2)
    wx_done.wait_recv()
    wz[u] = row_sum(wx, ng)
    for peer in u_peers:
        remote(wz.at[u], wz.at[u], s_m.at[4], r_m.at[4], peer).start()

    gz_done = whole(gz, nu - 1, 3)
    gz_done.wait_recv()
    hi, lo = pair_sum(gz, nu)
    ga[snaps, 0], ga[snaps, 1] = hi, lo
    for peer in snap_peers:
        remote(ga.at[snaps], ga.at[snaps], s_m.at[5], r_m.at[5], peer).start()
    ga_done = whole(ga, 7, 5)
    ga_done.wait_recv()

    for r in range(8):
        gt[0, r : r + 1, :] = ga[r, 0]
        gt[1, r : r + 1, :] = ga[r, 1]
    lane8 = lax.broadcasted_iota(jnp.int32, (8, 128), 1)
    sub8 = lax.broadcasted_iota(jnp.int32, (8, 128), 0)
    tiles_h, tiles_l = [], []
    for i in range(4):
        eye = jnp.where(lane8 - n == sub8 + 8 * i, 1.0, 0.0)
        turned_h = gt[0] if i == 0 else pltpu.roll(gt[0], 128 - n * i, 1)
        turned_l = gt[1] if i == 0 else pltpu.roll(gt[1], 128 - n * i, 1)
        tiles_h.append(jnp.where(lane8 < n, turned_h, eye))
        tiles_l.append(jnp.where(lane8 < n, turned_l, 0.0))
    factor = jnp.concatenate(eliminate(tiles_h, tiles_l), axis=0)

    wz_done = whole(wz, nu - 1, 4)
    wz_done.wait_recv()
    wa[g] = row_sum(wz, nu)
    for peer in g_peers:
        remote(wa.at[g], wa.at[g], s_m.at[6], r_m.at[6], peer).start()

    f_h, f_m, f_l = thirds(factor)
    f_h, f_m, f_l = f_h.astype(F32), f_m.astype(F32), f_l.astype(F32)
    which = lax.broadcasted_iota(jnp.int32, (n, 128), 1) // n
    left = jnp.where(
        which == 0, pltpu.roll(f_h, 96, 1),
        jnp.where(which == 1, f_h, jnp.where(which == 2, pltpu.roll(f_h, 32, 1), pltpu.roll(f_m, 64, 1))),
    )
    right = jnp.where(which == 0, pltpu.roll(f_m, 96, 1), f_l)
    inv_cat = jnp.concatenate([left, right[:, : 2 * n]], axis=1).astype(BF16)
    root = math.sqrt(total_cells)
    writes = []
    for q in range(8):
        columns = slice(q * ch, (q + 1) * ch)
        out_b[:, columns] = dot(inv_cat, s_cat[q]) * root
        writes.append(
            pltpu.make_async_copy(out_b.at[:, columns], basis_ref.at[:, columns], out_sem.at[q])
        )
        writes[-1].start()

    wa_done = whole(wa, ng - 1, 6)
    wa_done.wait_recv()
    w_total = jnp.concatenate([wa[i] for i in range(ng)], axis=0)
    t_h, t_m, t_l = thirds(w_total)
    out_c[...] = dot(inv_cat, jnp.concatenate([t_h, t_m, t_l, t_h, t_m, t_h], axis=0))
    writes.append(pltpu.make_async_copy(out_c, coef_ref, out_sem.at[8]))
    writes[-1].start()

    for copy in swaps + [b_up, b_down] + c_up + c_down + gathers + [f_up, f_down] + passes:
        copy.wait_send()
    for copy in (gs_done, gx_done, wx_done, gz_done, wz_done, ga_done, wa_done):
        copy.wait_send()
    for copy in writes:
        copy.wait()


def shards(snapshots, sketch):
    cells, snaps = snapshots.shape
    n = sketch.shape[1]
    nz = lax.axis_size("cells") // NX
    ch = cells // 8
    total = cells * lax.axis_size("cells")
    share = n // (2 * NX)
    dma = pltpu.SemaphoreType.DMA
    vm = pltpu.VMEM
    return pl.pallas_call(
        functools.partial(kernel, nz, ch, total),
        out_shape=(
            jax.ShapeDtypeStruct((n, cells), F32),
            jax.ShapeDtypeStruct((n, snaps), F32),
        ),
        in_specs=[
            pl.BlockSpec(memory_space=pl.ANY),
            pl.BlockSpec(memory_space=pltpu.VMEM),
        ],
        out_specs=(
            pl.BlockSpec(memory_space=pl.ANY),
            pl.BlockSpec(memory_space=pl.ANY),
        ),
        scratch_shapes=[
            vm((8, ch, snaps), F32),
            vm((8, ch, snaps), BF16), vm((8, ch, snaps), BF16), vm((8, ch, snaps), BF16),
            vm((4, n, ch), F32), vm((4, n, ch), F32),
            vm((n, ch), F32), vm((2, n // 2, ch), F32),
            vm((2, n, ch), F32), vm((2, n, ch), F32),
            vm((8, n, ch), F32), vm((8, 6 * n, ch), BF16),
            vm((8, 2, 1, 128), F32), vm((8, 2, 1, 128), F32),
            vm((2 * NX, 2, 1, 128), F32), vm((nz // 2, 2, 1, 128), F32),
            vm((8, 2, 1, 128), F32), vm((2, 8, 128), F32),
            vm((2 * NX, share, snaps), F32), vm((2 * NX, share, snaps), F32),
            vm((nz // 2, share, snaps), F32), vm((2 * NX, share, snaps), F32),
            vm((n, cells), F32), vm((n, snaps), F32),
            dma((8,)), dma((4,)), dma((4,)), dma((2,)), dma((2,)), dma((4,)), dma((4,)),
            dma((4,)), dma((4,)), dma((2,)), dma((2,)), dma((4,)), dma((4,)),
            dma((7,)), dma((7,)), dma((9,)), pltpu.SemaphoreType.REGULAR((2,)),
        ],
        compiler_params=pltpu.CompilerParams(collective_id=0, has_side_effects=True),
    )(snapshots, jnp.transpose(sketch))


def solution(mesh):
    return jax.shard_map(
        shards,
        mesh=mesh,
        in_specs=(P("cells", "snaps"), P("snaps", None)),
        out_specs=(P(None, "cells"), P(None, "snaps")),
        check_vma=False,
    )
```

```python
import functools
import math

import jax
import jax.numpy as jnp
from jax import lax
from jax.experimental import pallas as pl
from jax.experimental.pallas import tpu as pltpu
from jax.sharding import PartitionSpec as P

MESH = pl.DeviceIdType.MESH
NX = 4
F32 = jnp.float32
BF16 = jnp.bfloat16
ROWS = 32


def two_sum(a, b):
    s = a + b
    t = s - a
    return s, (a - (s - t)) + (b - t)


def quick_two_sum(a, b):
    s = a + b
    return s, b - (s - a)


def halves(a):
    c = a * 4097.0
    high = c - (c - a)
    return high, a - high


def two_prod(a, ah, al, b, bh, bl):
    p = a * b
    return p, ((ah * bh - p) + ah * bl + al * bh) + al * bl


def dd_add(ah, al, bh, bl):
    s, e = two_sum(ah, bh)
    return quick_two_sum(s, e + (al + bl))


def thirds(a):
    h = a.astype(BF16)
    rest = a - h.astype(F32)
    m = rest.astype(BF16)
    low = (rest - m.astype(F32)).astype(BF16)
    return h, m, low


def dot(a, b, transposed=False):
    dims = (((1,), (1 if transposed else 0,)), ((), ()))
    return lax.dot_general(a, b, dims, preferred_element_type=F32)


def six(lhs, h, m, low, transposed):
    n = ROWS
    dh = dot(lhs, h, transposed)
    dm = dot(lhs[: 2 * n], m, transposed)
    dl = dot(lhs[:n], low, transposed)
    small = (dh[2 * n :] + dm[n:]) + dl
    return dh[:n] + ((dh[n : 2 * n] + dm[:n]) + small)


def sum_pairs(pairs):
    while len(pairs) > 1:
        pairs = [
            dd_add(*pairs[i], *pairs[i + 1]) if i + 1 < len(pairs) else pairs[i]
            for i in range(0, len(pairs), 2)
        ]
    return pairs[0]


def power_above(x):
    p = jnp.full(x.shape, 2.0**-63, F32)
    inverse = jnp.full(x.shape, 2.0**63, F32)
    for step in (64, 32, 16, 8, 4, 2, 1):
        larger = x >= p * (2.0**step)
        p = jnp.where(larger, p * (2.0**step), p)
        inverse = jnp.where(larger, inverse * (2.0**-step), inverse)
    return p * 2.0, inverse * 0.5


def eliminate(gh, gl, midway=None):
    gh, gl = list(gh), list(gl)
    tiles = len(gh)
    sub = lax.broadcasted_iota(jnp.int32, (8, 128), 0)
    lane = lax.broadcasted_iota(jnp.int32, (8, 128), 1)

    def across(tile, k):
        return jnp.broadcast_to(tile[:, k : k + 1], (8, 128))

    def down(tile, r):
        return jnp.broadcast_to(tile[r : r + 1, :], (8, 128))

    for k in range(8 * tiles - 1):
        if midway is not None and k == 24:
            midway()
        ib, kr = divmod(k, 8)
        columns = {t: (across(gh[t], k), across(gl[t], k)) for t in range(ib, tiles)}
        ph, plo = down(columns[ib][0], kr), down(columns[ib][1], kr)
        rh, rl = down(gh[ib], kr), down(gl[ib], kr)
        r = 1.0 / ph
        pa, pb = halves(ph)
        q1 = rh * r
        qa, qb = halves(q1)
        t, te = two_prod(q1, qa, qb, ph, pa, pb)
        rest = (rh - t) - te + (rl - q1 * plo)
        uh, ul = quick_two_sum(q1, rest * r)
        ua, ub = halves(uh)
        for t in range(ib if kr < 7 else ib + 1, tiles):
            ch, cl = columns[t]
            if t == ib:
                ch = jnp.where(sub > kr, ch, 0.0)
                cl = jnp.where(sub > kr, cl, 0.0)
            ca, cb = halves(ch)
            p, pe = two_prod(ch, ca, cb, uh, ua, ub)
            pe = pe + (ch * ul + cl * uh)
            s, e = two_sum(gh[t], -p)
            gh[t], gl[t] = quick_two_sum(s, e + (gl[t] - pe))
    out = []
    for t in range(tiles):
        at = lane == sub + 8 * t
        d = jnp.sum(jnp.where(at, gh[t], 0.0), axis=1, keepdims=True)
        y = lax.rsqrt(d)
        y = y * (1.5 - 0.5 * d * y * y)
        out.append((gh[t] + gl[t]) * y)
    return out


def packed_gram(rows):
    n = ROWS
    top = jnp.max(jnp.abs(rows), axis=1, keepdims=True)
    scale, inverse = power_above(jnp.broadcast_to(top, (n, 128)))
    v = rows * (inverse[:, 0:1] * 64.0)
    parts = []
    for a in range(4):
        whole = jnp.round(v)
        parts.append(whole.astype(BF16))
        v = (v - whole) * 128.0
    slices = jnp.concatenate(parts, axis=0)
    products = dot(slices, slices, True)
    wide = lax.broadcasted_iota(jnp.int32, (n, 128), 1)
    tall = lax.broadcasted_iota(jnp.int32, (n, 128), 0)
    group = wide // n
    weight = jnp.where(
        group == 0, 2.0**-12,
        jnp.where(group == 1, 2.0**-19, jnp.where(group == 2, 2.0**-26, 2.0**-33)),
    )
    gh, gl = two_sum(products[0:n] * weight, products[n : 2 * n] * (weight * 2.0**-7))
    for a in (2, 3):
        gh, gl = dd_add(gh, gl, products[a * n : (a + 1) * n] * (weight * 2.0 ** (-7 * a)), 0.0)
    for turn in (64, 32):
        gh, gl = dd_add(gh, gl, pltpu.roll(gh, turn, 1), pltpu.roll(gl, turn, 1))
    column_scale = jnp.sum(jnp.where(wide - n * group == tall, scale, 0.0), axis=0, keepdims=True)
    both = scale * column_scale
    gh, gl = gh * both, gl * both
    lanes = lax.broadcasted_iota(jnp.int32, (8, 128), 1) // n

    def pack(g):
        out = g[0:8]
        for i in range(1, 4):
            out = jnp.where(lanes == i, g[8 * i : 8 * i + 8], out)
        return out

    return pack(gh), pack(gl)


def kernel(
    nz, ch, total_cells,
    a_ref, w_ref, basis_ref, coef_ref,
    w_buf, a_buf, a_h, a_m, a_l,
    send_a, got_a, rs_a, rs_b, rs_c, rs_d, s_all, s_cat,
    go, gs, gx, gz, ga, gt,
    wp, wx, wz, wa, out_b, out_c,
    load_sem, s_a, r_a, s_b, r_b, s_c, r_c, s_y, r_y, s_f, r_f, s_p, r_p, s_m, r_m,
    out_sem, know_sem,
):
    cells = lax.axis_index("cells")
    snaps = lax.axis_index("snaps")
    n = ROWS
    ng, nu = 2 * NX, nz // 2
    z, x = lax.div(cells, NX), lax.rem(cells, NX)
    u, odd = lax.div(z, 2), lax.rem(z, 2)
    y, core = lax.div(snaps, 2), lax.rem(snaps, 2)
    g = 2 * x + odd
    up, down, far = lax.rem(y + 1, 4), lax.rem(y + 3, 4), lax.rem(y + 2, 4)
    mate = (cells, 2 * y + 1 - core)
    above = (cells, 2 * up + core)
    below = (cells, 2 * down + core)
    snap_of = [lax.rem(snaps + d, 8) for d in (4, 5, 3, 2, 6, 1, 7)]
    snap_peers = [(cells, s) for s in snap_of]
    g_of = [lax.rem(g + d, ng) for d in range(1, ng)]
    g_peers = [((2 * u + lax.rem(o, 2)) * NX + lax.div(o, 2), snaps) for o in g_of]

    def at_u(d):
        return ((2 * lax.rem(u + d, nu) + odd) * NX + x, snaps)

    u_peers = [at_u(d) for d in sorted(range(1, nu), key=lambda d: -min(d, nu - d))]

    def remote(src, dst, ss, rs, to):
        return pltpu.make_async_remote_copy(
            src_ref=src, dst_ref=dst, send_sem=ss, recv_sem=rs,
            device_id=to, device_id_type=MESH,
        )

    def signal(sem, to):
        pl.semaphore_signal(sem, inc=1, device_id=to, device_id_type=MESH)

    chunk_of = []
    for o in (far, up, down, y):
        chunk_of += [(1 - core) * 4 + o, core * 4 + o]
    w_load = pltpu.make_async_copy(w_ref, w_buf, load_sem.at[8])
    w_load.start()
    loads = []
    for i, q in enumerate(chunk_of):
        start = pl.multiple_of(q * ch, ch)
        loads.append(
            pltpu.make_async_copy(a_ref.at[pl.ds(start, ch), :], a_buf.at[i], load_sem.at[i])
        )
        loads[-1].start()

    barrier = pltpu.get_barrier_semaphore()
    near = [mate, above, below]
    near += [(z * NX + lax.rem(x + d, NX), snaps) for d in sorted({1, NX - 1}) if d % NX]
    near += [(lax.rem(z + d, nz) * NX + x, snaps) for d in sorted({1, nz - 1})]
    for peer in near:
        signal(barrier, peer)

    w_load.wait()
    w_h, w_m, w_l = thirds(w_buf[...])
    w_cat = jnp.concatenate([w_h, w_m, w_l], axis=0)

    def sketch_chunk(i):
        loads[i].wait()
        h, m, low = thirds(a_buf[i])
        a_h[i], a_m[i], a_l[i] = h, m, low
        return six(w_cat, h, m, low, True)

    swaps = []

    def swap(j):
        swaps.append(remote(send_a.at[j], got_a.at[j], s_a.at[j], r_a.at[j], mate))
        swaps[-1].start()

    rounds = [near, near]
    reach = 1
    while reach < nu // 2:
        rounds.append([at_u(reach), at_u(nu - reach)])
        reach *= 2

    def tell(i):
        for peer in rounds[i] if i < len(rounds) else ():
            signal(know_sem.at[i], peer)

    def hear(i):
        if i < len(rounds):
            pl.semaphore_wait(know_sem.at[i], len(rounds[i]))

    send_a[0] = sketch_chunk(0)
    far_part = sketch_chunk(1)
    send_a[1] = sketch_chunk(2)
    up_part = sketch_chunk(3)
    pl.semaphore_wait(barrier, len(near))
    swap(0)
    swap(1)
    tell(0)
    send_a[2] = sketch_chunk(4)
    swap(2)
    swaps[0].wait_recv()
    rs_a[...] = far_part + got_a[0]
    b_up = remote(rs_a.at[0:16], rs_b.at[0], s_b.at[0], r_b.at[0], above)
    b_up.start()
    b_down = remote(rs_a.at[16:32], rs_b.at[1], s_b.at[1], r_b.at[1], below)
    b_down.start()
    hear(0)
    tell(1)
    down_part = sketch_chunk(5)
    swaps[1].wait_recv()
    up_part = up_part + got_a[1]
    rs_c[0, 16:32] = up_part[16:32]
    c_up = [remote(rs_c.at[0, 16:32], rs_d.at[0, 16:32], s_c.at[0], r_c.at[0], above)]
    c_up[0].start()
    send_a[3] = sketch_chunk(6)
    swap(3)
    swaps[2].wait_recv()
    down_part = down_part + got_a[2]
    rs_c[1, 0:16] = down_part[0:16]
    c_down = [remote(rs_c.at[1, 0:16], rs_d.at[1, 0:16], s_c.at[1], r_c.at[1], below)]
    c_down[0].start()
    own_part = sketch_chunk(7)
    hear(1)
    tell(2)
    b_up.wait_recv()
    rs_c[0, 0:16] = up_part[0:16] + rs_b[0]
    c_up.append(remote(rs_c.at[0, 0:16], rs_d.at[0, 0:16], s_c.at[2], r_c.at[2], above))
    c_up[1].start()
    b_down.wait_recv()
    rs_c[1, 16:32] = down_part[16:32] + rs_b[1]
    c_down.append(remote(rs_c.at[1, 16:32], rs_d.at[1, 16:32], s_c.at[3], r_c.at[3], below))
    c_down[1].start()
    swaps[3].wait_recv()
    own_part = own_part + got_a[3]
    hear(2)
    tell(3)
    for copy in c_up + c_down:
        copy.wait_recv()
    own = core * 4 + y
    own_rows = own_part + rs_d[0] + rs_d[1]
    s_all[own] = own_rows

    first, second = pl.ds(0, 16), pl.ds(16, 16)

    def along(slot, rows, sem, to, s, r):
        piece = s_all.at[slot, rows]
        return remote(piece, piece, s.at[sem], r.at[sem], to)

    gathers = [
        along(own, first, 0, above, s_y, r_y),
        along(own, second, 1, below, s_y, r_y),
        along(own, second, 2, above, s_y, r_y),
        along(own, first, 3, below, s_y, r_y),
    ]
    for copy in gathers:
        copy.start()

    passes = []

    def pass_on(slot):
        sem = len(passes)
        copy = remote(s_all.at[slot], s_all.at[slot], s_p.at[sem], r_p.at[sem], mate)
        copy.start()
        passes.append(copy)

    pass_on(own)

    gram_h, gram_l = packed_gram(own_rows)
    for r in range(8):
        go[r, 0] = gram_h[r : r + 1]
        go[r, 1] = gram_l[r : r + 1]
    gs[snaps] = go[snaps]
    for s, peer in zip(snap_of, snap_peers):
        remote(go.at[s], gs.at[snaps], s_m.at[0], r_m.at[0], peer).start()

    def whole(buf, count, sem):
        piece = buf.at[pl.ds(0, count)]
        return remote(piece, piece, s_m.at[sem], r_m.at[sem], mate)

    def pair_sum(buf, count):
        return sum_pairs([(buf[i, 0], buf[i, 1]) for i in range(count)])

    def row_sum(buf, count):
        rows = [buf[i] for i in range(count)]
        while len(rows) > 1:
            rows = [rows[i] + rows[i + 1] for i in range(0, len(rows), 2)]
        return rows[0]

    def projected(i, slot):
        s_h, s_m, s_l = thirds(s_all[slot])
        s_cat[slot, 0:n] = s_h
        s_cat[slot, n : 2 * n] = s_m
        s_cat[slot, 2 * n : 3 * n] = s_l
        s_cat[slot, 3 * n : 4 * n] = s_h
        s_cat[slot, 4 * n : 5 * n] = s_m
        s_cat[slot, 5 * n : 6 * n] = s_h
        lhs = jnp.concatenate([s_h, s_m, s_l], axis=0)
        return six(lhs, a_h[i], a_m[i], a_l[i], False)

    theirs = (1 - core) * 4
    slot_down, slot_up, slot_far = core * 4 + down, core * 4 + up, core * 4 + far
    w_sum = projected(7, own)
    passes[0].wait_recv()
    w_sum += projected(6, theirs + y)
    along(slot_down, first, 0, above, s_y, r_y).wait_recv()
    f_up = along(slot_down, first, 0, above, s_f, r_f)
    f_up.start()
    along(slot_up, second, 1, below, s_y, r_y).wait_recv()
    f_down = along(slot_up, second, 1, below, s_f, r_f)
    f_down.start()
    along(slot_down, second, 2, above, s_y, r_y).wait_recv()
    pass_on(slot_down)
    along(slot_up, first, 3, below, s_y, r_y).wait_recv()
    pass_on(slot_up)

    gs_done = whole(gs, 7, 0)
    gs_done.wait_recv()
    hi, lo = pair_sum(gs, 8)
    gx[g, 0], gx[g, 1] = hi, lo
    for peer in g_peers:
        remote(gx.at[g], gx.at[g], s_m.at[1], r_m.at[1], peer).start()

    w_sum += projected(5, slot_down)
    w_sum += projected(3, slot_up)
    f_up.wait_recv()
    f_down.wait_recv()
    pass_on(slot_far)
    passes[1].wait_recv()
    w_sum += projected(4, theirs + down)
    passes[2].wait_recv()
    w_sum += projected(2, theirs + up)
    w_sum += projected(1, slot_far)

    hear(3)
    gx_done = whole(gx, ng - 1, 1)
    gx_done.wait_recv()
    hi, lo = pair_sum(gx, ng)
    gz[u, 0], gz[u, 1] = hi, lo
    for peer in u_peers:
        remote(gz.at[u], gz.at[u], s_m.at[3], r_m.at[3], peer).start()

    passes[3].wait_recv()
    w_sum += projected(0, theirs + far)

    share = n // ng
    for i in range(ng):
        wp[i] = w_sum[i * share : (i + 1) * share]
    wx[g] = wp[g]
    for o, peer in zip(g_of, g_peers):
        remote(wp.at[o], wx.at[g], s_m.at[2], r_m.at[2], peer).start()

    wx_done = whole(wx, ng - 1, 2)
    wx_done.wait_recv()
    wz[u] = row_sum(wx, ng)
    for peer in u_peers:
        remote(wz.at[u], wz.at[u], s_m.at[4], r_m.at[4], peer).start()

    gz_done = whole(gz, nu - 1, 3)
    gz_done.wait_recv()
    hi, lo = pair_sum(gz, nu)
    ga[snaps, 0], ga[snaps, 1] = hi, lo
    for peer in snap_peers:
        remote(ga.at[snaps], ga.at[snaps], s_m.at[5], r_m.at[5], peer).start()
    ga_done = whole(ga, 7, 5)
    ga_done.wait_recv()

    for r in range(8):
        gt[0, r : r + 1, :] = ga[r, 0]
        gt[1, r : r + 1, :] = ga[r, 1]
    lane8 = lax.broadcasted_iota(jnp.int32, (8, 128), 1)
    sub8 = lax.broadcasted_iota(jnp.int32, (8, 128), 0)
    tiles_h, tiles_l = [], []
    for i in range(4):
        eye = jnp.where(lane8 - n == sub8 + 8 * i, 1.0, 0.0)
        turned_h = gt[0] if i == 0 else pltpu.roll(gt[0], 128 - n * i, 1)
        turned_l = gt[1] if i == 0 else pltpu.roll(gt[1], 128 - n * i, 1)
        tiles_h.append(jnp.where(lane8 < n, turned_h, eye))
        tiles_l.append(jnp.where(lane8 < n, turned_l, 0.0))
    wz_done = whole(wz, nu - 1, 4)

    def share_w():
        wz_done.wait_recv()
        wa[g] = row_sum(wz, nu)
        for peer in g_peers:
            remote(wa.at[g], wa.at[g], s_m.at[6], r_m.at[6], peer).start()

    factor = jnp.concatenate(eliminate(tiles_h, tiles_l, share_w), axis=0)

    f_h, f_m, f_l = thirds(factor)
    f_h, f_m, f_l = f_h.astype(F32), f_m.astype(F32), f_l.astype(F32)
    which = lax.broadcasted_iota(jnp.int32, (n, 128), 1) // n
    left = jnp.where(
        which == 0, pltpu.roll(f_h, 96, 1),
        jnp.where(which == 1, f_h, jnp.where(which == 2, pltpu.roll(f_h, 32, 1), pltpu.roll(f_m, 64, 1))),
    )
    right = jnp.where(which == 0, pltpu.roll(f_m, 96, 1), f_l)
    inv_cat = jnp.concatenate([left, right[:, : 2 * n]], axis=1).astype(BF16)
    root = math.sqrt(total_cells)
    writes = []
    for q in range(8):
        columns = slice(q * ch, (q + 1) * ch)
        out_b[:, columns] = dot(inv_cat, s_cat[q]) * root
        writes.append(
            pltpu.make_async_copy(out_b.at[:, columns], basis_ref.at[:, columns], out_sem.at[q])
        )
        writes[-1].start()

    wa_done = whole(wa, ng - 1, 6)
    wa_done.wait_recv()
    w_total = jnp.concatenate([wa[i] for i in range(ng)], axis=0)
    t_h, t_m, t_l = thirds(w_total)
    out_c[...] = dot(inv_cat, jnp.concatenate([t_h, t_m, t_l, t_h, t_m, t_h], axis=0))
    writes.append(pltpu.make_async_copy(out_c, coef_ref, out_sem.at[8]))
    writes[-1].start()

    for copy in swaps + [b_up, b_down] + c_up + c_down + gathers + [f_up, f_down] + passes:
        copy.wait_send()
    for copy in (gs_done, gx_done, wx_done, gz_done, wz_done, ga_done, wa_done):
        copy.wait_send()
    for copy in writes:
        copy.wait()


def deliver(*arrays):
    count = len(arrays)

    def body(*refs):
        copies = [
            pltpu.make_async_copy(refs[i], refs[count + i], refs[-1].at[i]) for i in range(count)
        ]
        for copy in copies:
            copy.start()
        for copy in copies:
            copy.wait()

    return pl.pallas_call(
        body,
        out_shape=tuple(jax.ShapeDtypeStruct(a.shape, a.dtype) for a in arrays),
        in_specs=[pl.BlockSpec(memory_space=pl.ANY)] * count,
        out_specs=(pl.BlockSpec(memory_space=pl.ANY),) * count,
        scratch_shapes=[pltpu.SemaphoreType.DMA((count,))],
        compiler_params=pltpu.CompilerParams(vmem_limit_bytes=1 << 20),
    )(*arrays)


def shards(snapshots, sketch):
    cells, snaps = snapshots.shape
    n = sketch.shape[1]
    nz = lax.axis_size("cells") // NX
    ch = cells // 8
    total = cells * lax.axis_size("cells")
    share = n // (2 * NX)
    dma = pltpu.SemaphoreType.DMA
    vm = pltpu.VMEM
    basis, coefficients = pl.pallas_call(
        functools.partial(kernel, nz, ch, total),
        out_shape=(
            jax.ShapeDtypeStruct((n, cells), F32),
            jax.ShapeDtypeStruct((n, snaps), F32),
        ),
        in_specs=[
            pl.BlockSpec(memory_space=pltpu.HBM),
            pl.BlockSpec(memory_space=pltpu.HBM),
        ],
        out_specs=(
            pl.BlockSpec(memory_space=pl.ANY),
            pl.BlockSpec(memory_space=pl.ANY),
        ),
        scratch_shapes=[
            vm((n, snaps), F32), vm((8, ch, snaps), F32),
            vm((8, ch, snaps), BF16), vm((8, ch, snaps), BF16), vm((8, ch, snaps), BF16),
            vm((4, n, ch), F32), vm((4, n, ch), F32),
            vm((n, ch), F32), vm((2, n // 2, ch), F32),
            vm((2, n, ch), F32), vm((2, n, ch), F32),
            vm((8, n, ch), F32), vm((8, 6 * n, ch), BF16),
            vm((8, 2, 1, 128), F32), vm((8, 2, 1, 128), F32),
            vm((2 * NX, 2, 1, 128), F32), vm((nz // 2, 2, 1, 128), F32),
            vm((8, 2, 1, 128), F32), vm((2, 8, 128), F32),
            vm((2 * NX, share, snaps), F32), vm((2 * NX, share, snaps), F32),
            vm((nz // 2, share, snaps), F32), vm((2 * NX, share, snaps), F32),
            vm((n, cells), F32), vm((n, snaps), F32),
            dma((9,)), dma((4,)), dma((4,)), dma((2,)), dma((2,)), dma((4,)), dma((4,)),
            dma((4,)), dma((4,)), dma((2,)), dma((2,)), dma((4,)), dma((4,)),
            dma((7,)), dma((7,)), dma((9,)), pltpu.SemaphoreType.REGULAR((4,)),
        ],
        compiler_params=pltpu.CompilerParams(
            collective_id=0, has_side_effects=True, vmem_limit_bytes=52 << 20
        ),
    )(snapshots, jnp.transpose(sketch))
    return deliver(basis, coefficients)


def solution(mesh):
    return jax.shard_map(
        shards,
        mesh=mesh,
        in_specs=(P("cells", "snaps"), P("snaps", None)),
        out_specs=(P(None, "cells"), P(None, "snaps")),
        check_vma=False,
    )
```

```python
import functools
import math

import jax
import jax.numpy as jnp
from jax import lax
from jax.experimental import pallas as pl
from jax.experimental.pallas import tpu as pltpu
from jax.sharding import PartitionSpec as P

MESH = pl.DeviceIdType.MESH
NX = 4
F32 = jnp.float32
BF16 = jnp.bfloat16
ROWS = 32


def two_sum(a, b):
    s = a + b
    t = s - a
    return s, (a - (s - t)) + (b - t)


def quick_two_sum(a, b):
    s = a + b
    return s, b - (s - a)


def halves(a):
    c = a * 4097.0
    high = c - (c - a)
    return high, a - high


def two_prod(a, ah, al, b, bh, bl):
    p = a * b
    return p, ((ah * bh - p) + ah * bl + al * bh) + al * bl


def dd_add(ah, al, bh, bl):
    s, e = two_sum(ah, bh)
    return quick_two_sum(s, e + (al + bl))


def thirds(a):
    h = a.astype(BF16)
    rest = a - h.astype(F32)
    m = rest.astype(BF16)
    low = (rest - m.astype(F32)).astype(BF16)
    return h, m, low


def dot(a, b, transposed=False):
    dims = (((1,), (1 if transposed else 0,)), ((), ()))
    return lax.dot_general(a, b, dims, preferred_element_type=F32)


def six(lhs, h, m, low, transposed):
    n = ROWS
    dh = dot(lhs, h, transposed)
    dm = dot(lhs[: 2 * n], m, transposed)
    dl = dot(lhs[:n], low, transposed)
    small = (dh[2 * n :] + dm[n:]) + dl
    return dh[:n] + ((dh[n : 2 * n] + dm[:n]) + small)


def sum_pairs(pairs):
    while len(pairs) > 1:
        pairs = [
            dd_add(*pairs[i], *pairs[i + 1]) if i + 1 < len(pairs) else pairs[i]
            for i in range(0, len(pairs), 2)
        ]
    return pairs[0]


def power_above(x):
    p = jnp.full(x.shape, 2.0**-63, F32)
    inverse = jnp.full(x.shape, 2.0**63, F32)
    for step in (64, 32, 16, 8, 4, 2, 1):
        larger = x >= p * (2.0**step)
        p = jnp.where(larger, p * (2.0**step), p)
        inverse = jnp.where(larger, inverse * (2.0**-step), inverse)
    return p * 2.0, inverse * 0.5


def eliminate(gh, gl, midway=None, block=4):
    gh, gl = list(gh), list(gl)
    tiles = len(gh)
    last = 8 * tiles - 1
    sub = lax.broadcasted_iota(jnp.int32, (8, 128), 0)
    lane = lax.broadcasted_iota(jnp.int32, (8, 128), 1)

    def across(tile, k):
        return jnp.broadcast_to(tile[:, k : k + 1], (8, 128))

    def down(tile, r):
        return jnp.broadcast_to(tile[r : r + 1, :], (8, 128))

    for start in range(0, last, block):
        if midway is not None and start == 16:
            midway()
        ib = start // 8
        columns = [
            {t: (across(gh[t], k), across(gl[t], k)) for t in range(ib, tiles)}
            for k in range(start, start + block)
        ]
        for j in range(block):
            k, kr = start + j, (start + j) % 8
            if k == last:
                break
            ph, plo = (down(v, kr) for v in columns[j][ib])
            r = 1.0 / ph
            ra, rb = halves(r)

            def scaled(h, low):
                ha, hb = halves(h)
                p, e = two_prod(h, ha, hb, r, ra, rb)
                return p, e + low * r

            one, rest = scaled(ph, plo)
            slip = (one - 1.0) + rest
            uh, ul = scaled(down(gh[ib], kr), down(gl[ib], kr))
            rows = [(uh, ul) + halves(uh)]
            for i in range(j + 1, block):
                vh, vl = scaled(*(down(v, kr) for v in columns[i][ib]))
                rows.append((vh, vl) + halves(vh))
            for t in range(ib if kr < 7 else ib + 1, tiles):
                ch, cl = columns[j][t]
                slip_t = slip
                if t == ib:
                    ch = jnp.where(sub > kr, ch, 0.0)
                    cl = jnp.where(sub > kr, cl, 0.0)
                    slip_t = jnp.where(sub > kr, slip, 0.0)
                ca, cb = halves(ch)

                def reduced(h, low, row):
                    vh, vl, va, vb = row
                    p, e = two_prod(ch, ca, cb, vh, va, vb)
                    e = (ch * vl + cl * vh) + e
                    s, d = two_sum(h, -p)
                    return quick_two_sum(s, d + ((low + h * slip_t) - e))

                gh[t], gl[t] = reduced(gh[t], gl[t], rows[0])
                for i in range(j + 1, block):
                    columns[i][t] = reduced(*columns[i][t], rows[i - j])
    out = []
    for t in range(tiles):
        at = lane == sub + 8 * t
        d = jnp.sum(jnp.where(at, gh[t], 0.0), axis=1, keepdims=True)
        y = lax.rsqrt(d)
        y = y * (1.5 - 0.5 * d * y * y)
        out.append((gh[t] + gl[t]) * y)
    return out


def packed_gram(rows):
    n = ROWS
    top = jnp.max(jnp.abs(rows), axis=1, keepdims=True)
    scale, inverse = power_above(jnp.broadcast_to(top, (n, 128)))
    v = rows * (inverse[:, 0:1] * 64.0)
    parts = []
    for a in range(4):
        whole = jnp.round(v)
        parts.append(whole.astype(BF16))
        v = (v - whole) * 128.0
    slices = jnp.concatenate(parts, axis=0)
    products = dot(slices, slices, True)
    wide = lax.broadcasted_iota(jnp.int32, (n, 128), 1)
    tall = lax.broadcasted_iota(jnp.int32, (n, 128), 0)
    group = wide // n
    weight = jnp.where(
        group == 0, 2.0**-12,
        jnp.where(group == 1, 2.0**-19, jnp.where(group == 2, 2.0**-26, 2.0**-33)),
    )
    gh, gl = two_sum(products[0:n] * weight, products[n : 2 * n] * (weight * 2.0**-7))
    for a in (2, 3):
        gh, gl = dd_add(gh, gl, products[a * n : (a + 1) * n] * (weight * 2.0 ** (-7 * a)), 0.0)
    for turn in (64, 32):
        gh, gl = dd_add(gh, gl, pltpu.roll(gh, turn, 1), pltpu.roll(gl, turn, 1))
    column_scale = jnp.sum(jnp.where(wide - n * group == tall, scale, 0.0), axis=0, keepdims=True)
    both = scale * column_scale
    gh, gl = gh * both, gl * both
    lanes = lax.broadcasted_iota(jnp.int32, (8, 128), 1) // n

    def pack(g):
        out = g[0:8]
        for i in range(1, 4):
            out = jnp.where(lanes == i, g[8 * i : 8 * i + 8], out)
        return out

    return pack(gh), pack(gl)


def kernel(
    nz, ch, total_cells,
    a_ref, w_ref, basis_ref, coef_ref,
    w_buf, a_buf, a_h, a_m, a_l,
    send_a, got_a, rs_a, rs_b, rs_c, rs_d, s_all, s_cat,
    go, gs, gx, gz, ga, gt,
    wp, wx, wz, wa, out_b, out_c,
    load_sem, s_a, r_a, s_b, r_b, s_c, r_c, s_y, r_y, s_f, r_f, s_p, r_p, s_m, r_m,
    out_sem, know_sem,
):
    cells = lax.axis_index("cells")
    snaps = lax.axis_index("snaps")
    n = ROWS
    ng, nu = 2 * NX, nz // 2
    z, x = lax.div(cells, NX), lax.rem(cells, NX)
    u, odd = lax.div(z, 2), lax.rem(z, 2)
    y, core = lax.div(snaps, 2), lax.rem(snaps, 2)
    g = 2 * x + odd
    up, down, far = lax.rem(y + 1, 4), lax.rem(y + 3, 4), lax.rem(y + 2, 4)
    mate = (cells, 2 * y + 1 - core)
    above = (cells, 2 * up + core)
    below = (cells, 2 * down + core)
    snap_of = [lax.rem(snaps + d, 8) for d in (4, 5, 3, 2, 6, 1, 7)]
    snap_peers = [(cells, s) for s in snap_of]
    g_of = [lax.rem(g + d, ng) for d in range(1, ng)]
    g_peers = [((2 * u + lax.rem(o, 2)) * NX + lax.div(o, 2), snaps) for o in g_of]

    def at_u(d):
        return ((2 * lax.rem(u + d, nu) + odd) * NX + x, snaps)

    u_peers = [at_u(d) for d in sorted(range(1, nu), key=lambda d: -min(d, nu - d))]

    def remote(src, dst, ss, rs, to):
        return pltpu.make_async_remote_copy(
            src_ref=src, dst_ref=dst, send_sem=ss, recv_sem=rs,
            device_id=to, device_id_type=MESH,
        )

    def signal(sem, to):
        pl.semaphore_signal(sem, inc=1, device_id=to, device_id_type=MESH)

    chunk_of = []
    for o in (far, up, down, y):
        chunk_of += [(1 - core) * 4 + o, core * 4 + o]
    w_load = pltpu.make_async_copy(w_ref, w_buf, load_sem.at[8])
    w_load.start()
    loads = []
    for i, q in enumerate(chunk_of):
        start = pl.multiple_of(q * ch, ch)
        loads.append(
            pltpu.make_async_copy(a_ref.at[pl.ds(start, ch), :], a_buf.at[i], load_sem.at[i])
        )
        loads[-1].start()

    barrier = pltpu.get_barrier_semaphore()
    near = [mate, above, below]
    near += [(z * NX + lax.rem(x + d, NX), snaps) for d in sorted({1, NX - 1}) if d % NX]
    near += [(lax.rem(z + d, nz) * NX + x, snaps) for d in sorted({1, nz - 1})]
    for peer in near:
        signal(barrier, peer)

    w_load.wait()
    w_h, w_m, w_l = thirds(w_buf[...])
    w_cat = jnp.concatenate([w_h, w_m, w_l], axis=0)

    def sketch_chunk(i):
        loads[i].wait()
        h, m, low = thirds(a_buf[i])
        a_h[i], a_m[i], a_l[i] = h, m, low
        return six(w_cat, h, m, low, True)

    swaps = []

    def swap(j):
        swaps.append(remote(send_a.at[j], got_a.at[j], s_a.at[j], r_a.at[j], mate))
        swaps[-1].start()

    rounds = [near, near]
    reach = 1
    while reach < nu // 2:
        rounds.append([at_u(reach), at_u(nu - reach)])
        reach *= 2

    def tell(i):
        for peer in rounds[i] if i < len(rounds) else ():
            signal(know_sem.at[i], peer)

    def hear(i):
        if i < len(rounds):
            pl.semaphore_wait(know_sem.at[i], len(rounds[i]))

    send_a[0] = sketch_chunk(0)
    pl.semaphore_wait(barrier, len(near))
    swap(0)
    far_part = sketch_chunk(1)
    send_a[1] = sketch_chunk(2)
    swap(1)
    tell(0)
    swaps[0].wait_recv()
    rs_a[...] = far_part + got_a[0]
    b_up = remote(rs_a.at[0:16], rs_b.at[0], s_b.at[0], r_b.at[0], above)
    b_up.start()
    b_down = remote(rs_a.at[16:32], rs_b.at[1], s_b.at[1], r_b.at[1], below)
    b_down.start()
    up_part = sketch_chunk(3)
    send_a[2] = sketch_chunk(4)
    swap(2)
    hear(0)
    tell(1)
    down_part = sketch_chunk(5)
    swaps[1].wait_recv()
    up_part = up_part + got_a[1]
    rs_c[0, 16:32] = up_part[16:32]
    c_up = [remote(rs_c.at[0, 16:32], rs_d.at[0, 16:32], s_c.at[0], r_c.at[0], above)]
    c_up[0].start()
    send_a[3] = sketch_chunk(6)
    swap(3)
    swaps[2].wait_recv()
    down_part = down_part + got_a[2]
    rs_c[1, 0:16] = down_part[0:16]
    c_down = [remote(rs_c.at[1, 0:16], rs_d.at[1, 0:16], s_c.at[1], r_c.at[1], below)]
    c_down[0].start()
    own_part = sketch_chunk(7)
    hear(1)
    tell(2)
    b_up.wait_recv()
    rs_c[0, 0:16] = up_part[0:16] + rs_b[0]
    c_up.append(remote(rs_c.at[0, 0:16], rs_d.at[0, 0:16], s_c.at[2], r_c.at[2], above))
    c_up[1].start()
    b_down.wait_recv()
    rs_c[1, 16:32] = down_part[16:32] + rs_b[1]
    c_down.append(remote(rs_c.at[1, 16:32], rs_d.at[1, 16:32], s_c.at[3], r_c.at[3], below))
    c_down[1].start()
    swaps[3].wait_recv()
    own_part = own_part + got_a[3]
    hear(2)
    tell(3)
    for copy in c_up + c_down:
        copy.wait_recv()
    own = core * 4 + y
    own_rows = own_part + rs_d[0] + rs_d[1]
    s_all[own] = own_rows

    first, second = pl.ds(0, 16), pl.ds(16, 16)

    def along(slot, rows, sem, to, s, r):
        piece = s_all.at[slot, rows]
        return remote(piece, piece, s.at[sem], r.at[sem], to)

    gathers = [
        along(own, first, 0, above, s_y, r_y),
        along(own, second, 1, below, s_y, r_y),
        along(own, second, 2, above, s_y, r_y),
        along(own, first, 3, below, s_y, r_y),
    ]
    for copy in gathers:
        copy.start()

    passes = []

    def pass_on(slot):
        sem = len(passes)
        copy = remote(s_all.at[slot], s_all.at[slot], s_p.at[sem], r_p.at[sem], mate)
        copy.start()
        passes.append(copy)

    pass_on(own)

    gram_h, gram_l = packed_gram(own_rows)
    for r in range(8):
        go[r, 0] = gram_h[r : r + 1]
        go[r, 1] = gram_l[r : r + 1]
    gs[snaps] = go[snaps]
    for s, peer in zip(snap_of, snap_peers):
        remote(go.at[s], gs.at[snaps], s_m.at[0], r_m.at[0], peer).start()

    def whole(buf, count, sem):
        piece = buf.at[pl.ds(0, count)]
        return remote(piece, piece, s_m.at[sem], r_m.at[sem], mate)

    def pair_sum(buf, count):
        return sum_pairs([(buf[i, 0], buf[i, 1]) for i in range(count)])

    def row_sum(buf, count):
        rows = [buf[i] for i in range(count)]
        while len(rows) > 1:
            rows = [rows[i] + rows[i + 1] for i in range(0, len(rows), 2)]
        return rows[0]

    def projected(i, slot):
        s_h, s_m, s_l = thirds(s_all[slot])
        s_cat[slot, 0:n] = s_h
        s_cat[slot, n : 2 * n] = s_m
        s_cat[slot, 2 * n : 3 * n] = s_l
        s_cat[slot, 3 * n : 4 * n] = s_h
        s_cat[slot, 4 * n : 5 * n] = s_m
        s_cat[slot, 5 * n : 6 * n] = s_h
        lhs = jnp.concatenate([s_h, s_m, s_l], axis=0)
        return six(lhs, a_h[i], a_m[i], a_l[i], False)

    theirs = (1 - core) * 4
    slot_down, slot_up, slot_far = core * 4 + down, core * 4 + up, core * 4 + far
    w_sum = projected(7, own)
    passes[0].wait_recv()
    w_sum += projected(6, theirs + y)
    along(slot_down, first, 0, above, s_y, r_y).wait_recv()
    f_up = along(slot_down, first, 0, above, s_f, r_f)
    f_up.start()
    along(slot_up, second, 1, below, s_y, r_y).wait_recv()
    f_down = along(slot_up, second, 1, below, s_f, r_f)
    f_down.start()
    along(slot_down, second, 2, above, s_y, r_y).wait_recv()
    pass_on(slot_down)
    along(slot_up, first, 3, below, s_y, r_y).wait_recv()
    pass_on(slot_up)

    gs_done = whole(gs, 7, 0)
    gs_done.wait_recv()
    hi, lo = pair_sum(gs, 8)
    gx[g, 0], gx[g, 1] = hi, lo
    for peer in g_peers:
        remote(gx.at[g], gx.at[g], s_m.at[1], r_m.at[1], peer).start()

    w_sum += projected(5, slot_down)
    w_sum += projected(3, slot_up)
    f_up.wait_recv()
    f_down.wait_recv()
    pass_on(slot_far)
    passes[1].wait_recv()
    w_sum += projected(4, theirs + down)
    passes[2].wait_recv()
    w_sum += projected(2, theirs + up)
    w_sum += projected(1, slot_far)

    hear(3)
    gx_done = whole(gx, ng - 1, 1)
    gx_done.wait_recv()
    hi, lo = pair_sum(gx, ng)
    gz[u, 0], gz[u, 1] = hi, lo
    for peer in u_peers:
        remote(gz.at[u], gz.at[u], s_m.at[3], r_m.at[3], peer).start()

    passes[3].wait_recv()
    w_sum += projected(0, theirs + far)

    share = n // ng
    for i in range(ng):
        wp[i] = w_sum[i * share : (i + 1) * share]
    wx[g] = wp[g]
    for o, peer in zip(g_of, g_peers):
        remote(wp.at[o], wx.at[g], s_m.at[2], r_m.at[2], peer).start()

    wx_done = whole(wx, ng - 1, 2)
    wx_done.wait_recv()
    wz[u] = row_sum(wx, ng)
    for peer in u_peers:
        remote(wz.at[u], wz.at[u], s_m.at[4], r_m.at[4], peer).start()

    gz_done = whole(gz, nu - 1, 3)
    gz_done.wait_recv()
    hi, lo = pair_sum(gz, nu)
    ga[snaps, 0], ga[snaps, 1] = hi, lo
    for peer in snap_peers:
        remote(ga.at[snaps], ga.at[snaps], s_m.at[5], r_m.at[5], peer).start()
    ga_done = whole(ga, 7, 5)
    ga_done.wait_recv()

    for r in range(8):
        gt[0, r : r + 1, :] = ga[r, 0]
        gt[1, r : r + 1, :] = ga[r, 1]
    lane8 = lax.broadcasted_iota(jnp.int32, (8, 128), 1)
    sub8 = lax.broadcasted_iota(jnp.int32, (8, 128), 0)
    tiles_h, tiles_l = [], []
    for i in range(4):
        eye = jnp.where(lane8 - n == sub8 + 8 * i, 1.0, 0.0)
        turned_h = gt[0] if i == 0 else pltpu.roll(gt[0], 128 - n * i, 1)
        turned_l = gt[1] if i == 0 else pltpu.roll(gt[1], 128 - n * i, 1)
        tiles_h.append(jnp.where(lane8 < n, turned_h, eye))
        tiles_l.append(jnp.where(lane8 < n, turned_l, 0.0))
    wz_done = whole(wz, nu - 1, 4)

    def share_w():
        wz_done.wait_recv()
        wa[g] = row_sum(wz, nu)
        for peer in g_peers:
            remote(wa.at[g], wa.at[g], s_m.at[6], r_m.at[6], peer).start()

    factor = jnp.concatenate(eliminate(tiles_h, tiles_l, share_w), axis=0)

    f_h, f_m, f_l = thirds(factor)
    f_h, f_m, f_l = f_h.astype(F32), f_m.astype(F32), f_l.astype(F32)
    which = lax.broadcasted_iota(jnp.int32, (n, 128), 1) // n
    left = jnp.where(
        which == 0, pltpu.roll(f_h, 96, 1),
        jnp.where(which == 1, f_h, jnp.where(which == 2, pltpu.roll(f_h, 32, 1), pltpu.roll(f_m, 64, 1))),
    )
    right = jnp.where(which == 0, pltpu.roll(f_m, 96, 1), f_l)
    inv_cat = jnp.concatenate([left, right[:, : 2 * n]], axis=1).astype(BF16)
    root = math.sqrt(total_cells)
    writes = []
    for q in range(8):
        columns = slice(q * ch, (q + 1) * ch)
        out_b[:, columns] = dot(inv_cat, s_cat[q]) * root
        writes.append(
            pltpu.make_async_copy(out_b.at[:, columns], basis_ref.at[:, columns], out_sem.at[q])
        )
        writes[-1].start()

    wa_done = whole(wa, ng - 1, 6)
    wa_done.wait_recv()
    w_total = jnp.concatenate([wa[i] for i in range(ng)], axis=0)
    t_h, t_m, t_l = thirds(w_total)
    out_c[...] = dot(inv_cat, jnp.concatenate([t_h, t_m, t_l, t_h, t_m, t_h], axis=0))
    writes.append(pltpu.make_async_copy(out_c, coef_ref, out_sem.at[8]))
    writes[-1].start()

    for copy in swaps + [b_up, b_down] + c_up + c_down + gathers + [f_up, f_down] + passes:
        copy.wait_send()
    for copy in (gs_done, gx_done, wx_done, gz_done, wz_done, ga_done, wa_done):
        copy.wait_send()
    for copy in writes:
        copy.wait()


def deliver(*arrays):
    count = len(arrays)

    def body(*refs):
        copies = [
            pltpu.make_async_copy(refs[i], refs[count + i], refs[-1].at[i]) for i in range(count)
        ]
        for copy in copies:
            copy.start()
        for copy in copies:
            copy.wait()

    return pl.pallas_call(
        body,
        out_shape=tuple(jax.ShapeDtypeStruct(a.shape, a.dtype) for a in arrays),
        in_specs=[pl.BlockSpec(memory_space=pl.ANY)] * count,
        out_specs=(pl.BlockSpec(memory_space=pl.ANY),) * count,
        scratch_shapes=[pltpu.SemaphoreType.DMA((count,))],
        compiler_params=pltpu.CompilerParams(vmem_limit_bytes=1 << 20),
    )(*arrays)


def shards(snapshots, sketch):
    cells, snaps = snapshots.shape
    n = sketch.shape[1]
    nz = lax.axis_size("cells") // NX
    ch = cells // 8
    total = cells * lax.axis_size("cells")
    share = n // (2 * NX)
    dma = pltpu.SemaphoreType.DMA
    vm = pltpu.VMEM
    basis, coefficients = pl.pallas_call(
        functools.partial(kernel, nz, ch, total),
        out_shape=(
            jax.ShapeDtypeStruct((n, cells), F32),
            jax.ShapeDtypeStruct((n, snaps), F32),
        ),
        in_specs=[
            pl.BlockSpec(memory_space=pltpu.HBM),
            pl.BlockSpec(memory_space=pltpu.HBM),
        ],
        out_specs=(
            pl.BlockSpec(memory_space=pl.ANY),
            pl.BlockSpec(memory_space=pl.ANY),
        ),
        scratch_shapes=[
            vm((n, snaps), F32), vm((8, ch, snaps), F32),
            vm((8, ch, snaps), BF16), vm((8, ch, snaps), BF16), vm((8, ch, snaps), BF16),
            vm((4, n, ch), F32), vm((4, n, ch), F32),
            vm((n, ch), F32), vm((2, n // 2, ch), F32),
            vm((2, n, ch), F32), vm((2, n, ch), F32),
            vm((8, n, ch), F32), vm((8, 6 * n, ch), BF16),
            vm((8, 2, 1, 128), F32), vm((8, 2, 1, 128), F32),
            vm((2 * NX, 2, 1, 128), F32), vm((nz // 2, 2, 1, 128), F32),
            vm((8, 2, 1, 128), F32), vm((2, 8, 128), F32),
            vm((2 * NX, share, snaps), F32), vm((2 * NX, share, snaps), F32),
            vm((nz // 2, share, snaps), F32), vm((2 * NX, share, snaps), F32),
            vm((n, cells), F32), vm((n, snaps), F32),
            dma((9,)), dma((4,)), dma((4,)), dma((2,)), dma((2,)), dma((4,)), dma((4,)),
            dma((4,)), dma((4,)), dma((2,)), dma((2,)), dma((4,)), dma((4,)),
            dma((7,)), dma((7,)), dma((9,)), pltpu.SemaphoreType.REGULAR((4,)),
        ],
        compiler_params=pltpu.CompilerParams(
            collective_id=0, has_side_effects=True, vmem_limit_bytes=52 << 20
        ),
    )(snapshots, jnp.transpose(sketch))
    return deliver(basis, coefficients)


def solution(mesh):
    return jax.shard_map(
        shards,
        mesh=mesh,
        in_specs=(P("cells", "snaps"), P("snaps", None)),
        out_specs=(P(None, "cells"), P(None, "snaps")),
        check_vma=False,
    )
```

```python
import functools
import math

import jax
import jax.numpy as jnp
from jax import lax
from jax.experimental import pallas as pl
from jax.experimental.pallas import tpu as pltpu
from jax.sharding import PartitionSpec as P

MESH = pl.DeviceIdType.MESH
NX = 4
F32 = jnp.float32
BF16 = jnp.bfloat16
ROWS = 32


def two_sum(a, b):
    s = a + b
    t = s - a
    return s, (a - (s - t)) + (b - t)


def quick_two_sum(a, b):
    s = a + b
    return s, b - (s - a)


def halves(a):
    c = a * 4097.0
    high = c - (c - a)
    return high, a - high


def two_prod(a, ah, al, b, bh, bl):
    p = a * b
    return p, ((ah * bh - p) + ah * bl + al * bh) + al * bl


def dd_add(ah, al, bh, bl):
    s, e = two_sum(ah, bh)
    return quick_two_sum(s, e + (al + bl))


def thirds(a):
    h = a.astype(BF16)
    rest = a - h.astype(F32)
    m = rest.astype(BF16)
    low = (rest - m.astype(F32)).astype(BF16)
    return h, m, low


def dot(a, b, transposed=False):
    dims = (((1,), (1 if transposed else 0,)), ((), ()))
    return lax.dot_general(a, b, dims, preferred_element_type=F32)


def six(lhs, h, m, low, transposed):
    n = ROWS
    dh = dot(lhs, h, transposed)
    dm = dot(lhs[: 2 * n], m, transposed)
    dl = dot(lhs[:n], low, transposed)
    small = (dh[2 * n :] + dm[n:]) + dl
    return dh[:n] + ((dh[n : 2 * n] + dm[:n]) + small)


def sum_pairs(pairs):
    while len(pairs) > 1:
        pairs = [
            dd_add(*pairs[i], *pairs[i + 1]) if i + 1 < len(pairs) else pairs[i]
            for i in range(0, len(pairs), 2)
        ]
    return pairs[0]


def power_above(x):
    p = jnp.full(x.shape, 2.0**-63, F32)
    inverse = jnp.full(x.shape, 2.0**63, F32)
    for step in (64, 32, 16, 8, 4, 2, 1):
        larger = x >= p * (2.0**step)
        p = jnp.where(larger, p * (2.0**step), p)
        inverse = jnp.where(larger, inverse * (2.0**-step), inverse)
    return p * 2.0, inverse * 0.5


def eliminate(gh, gl, midway=None, block=4):
    gh, gl = list(gh), list(gl)
    tiles = len(gh)
    last = 8 * tiles - 1
    sub = lax.broadcasted_iota(jnp.int32, (8, 128), 0)
    lane = lax.broadcasted_iota(jnp.int32, (8, 128), 1)

    def across(tile, k):
        return jnp.broadcast_to(tile[:, k : k + 1], (8, 128))

    def down(tile, r):
        return jnp.broadcast_to(tile[r : r + 1, :], (8, 128))

    for start in range(0, last, block):
        if midway is not None and start == 16:
            midway()
        ib = start // 8
        columns = [
            {t: (across(gh[t], k), across(gl[t], k)) for t in range(ib, tiles)}
            for k in range(start, start + block)
        ]
        for j in range(block):
            k, kr = start + j, (start + j) % 8
            if k == last:
                break
            ph, plo = (down(v, kr) for v in columns[j][ib])
            r = 1.0 / ph
            ra, rb = halves(r)

            def scaled(h, low):
                ha, hb = halves(h)
                p, e = two_prod(h, ha, hb, r, ra, rb)
                return p, e + low * r

            one, rest = scaled(ph, plo)
            slip = (one - 1.0) + rest
            uh, ul = scaled(down(gh[ib], kr), down(gl[ib], kr))
            rows = [(uh, ul) + halves(uh)]
            for i in range(j + 1, block):
                vh, vl = scaled(*(down(v, kr) for v in columns[i][ib]))
                rows.append((vh, vl) + halves(vh))
            for t in range(ib if kr < 7 else ib + 1, tiles):
                ch, cl = columns[j][t]
                slip_t = slip
                if t == ib:
                    ch = jnp.where(sub > kr, ch, 0.0)
                    cl = jnp.where(sub > kr, cl, 0.0)
                    slip_t = jnp.where(sub > kr, slip, 0.0)
                ca, cb = halves(ch)

                def reduced(h, low, row):
                    vh, vl, va, vb = row
                    p, e = two_prod(ch, ca, cb, vh, va, vb)
                    e = (ch * vl + cl * vh) + e
                    s, d = two_sum(h, -p)
                    return quick_two_sum(s, d + ((low + h * slip_t) - e))

                gh[t], gl[t] = reduced(gh[t], gl[t], rows[0])
                for i in range(j + 1, block):
                    columns[i][t] = reduced(*columns[i][t], rows[i - j])
    out = []
    for t in range(tiles):
        at = lane == sub + 8 * t
        d = jnp.sum(jnp.where(at, gh[t], 0.0), axis=1, keepdims=True)
        y = lax.rsqrt(d)
        y = y * (1.5 - 0.5 * d * y * y)
        out.append((gh[t] + gl[t]) * y)
    return out


def packed_gram(rows):
    n = ROWS
    top = jnp.max(jnp.abs(rows), axis=1, keepdims=True)
    scale, inverse = power_above(jnp.broadcast_to(top, (n, 128)))
    v = rows * (inverse[:, 0:1] * 64.0)
    parts = []
    for a in range(4):
        whole = jnp.round(v)
        parts.append(whole.astype(BF16))
        v = (v - whole) * 128.0
    slices = jnp.concatenate(parts, axis=0)
    products = dot(slices, slices, True)
    wide = lax.broadcasted_iota(jnp.int32, (n, 128), 1)
    tall = lax.broadcasted_iota(jnp.int32, (n, 128), 0)
    group = wide // n
    weight = jnp.where(
        group == 0, 2.0**-12,
        jnp.where(group == 1, 2.0**-19, jnp.where(group == 2, 2.0**-26, 2.0**-33)),
    )
    gh, gl = two_sum(products[0:n] * weight, products[n : 2 * n] * (weight * 2.0**-7))
    for a in (2, 3):
        gh, gl = dd_add(gh, gl, products[a * n : (a + 1) * n] * (weight * 2.0 ** (-7 * a)), 0.0)
    for turn in (64, 32):
        gh, gl = dd_add(gh, gl, pltpu.roll(gh, turn, 1), pltpu.roll(gl, turn, 1))
    column_scale = jnp.sum(jnp.where(wide - n * group == tall, scale, 0.0), axis=0, keepdims=True)
    both = scale * column_scale
    gh, gl = gh * both, gl * both
    lanes = lax.broadcasted_iota(jnp.int32, (8, 128), 1) // n

    def pack(g):
        out = g[0:8]
        for i in range(1, 4):
            out = jnp.where(lanes == i, g[8 * i : 8 * i + 8], out)
        return out

    return pack(gh), pack(gl)


def kernel(
    nz, ch, total_cells,
    a_ref, w_ref, basis_ref, coef_ref,
    w_buf, a_buf, a_h, a_m, a_l,
    send_a, got_a, rs_a, rs_b, rs_c, rs_d, s_all, s_cat,
    go, gs, gx, gz, ga, gt,
    wp, wx, wz, wa, out_b, out_c,
    load_sem, s_a, r_a, s_b, r_b, s_c, r_c, s_y, r_y, s_f, r_f, s_p, r_p, s_m, r_m,
    out_sem, know_sem,
):
    cells = lax.axis_index("cells")
    snaps = lax.axis_index("snaps")
    n = ROWS
    ng, nu = 2 * NX, nz // 2
    z, x = lax.div(cells, NX), lax.rem(cells, NX)
    u, odd = lax.div(z, 2), lax.rem(z, 2)
    y, core = lax.div(snaps, 2), lax.rem(snaps, 2)
    g = 2 * x + odd
    up, down, far = lax.rem(y + 1, 4), lax.rem(y + 3, 4), lax.rem(y + 2, 4)
    mate = (cells, 2 * y + 1 - core)
    above = (cells, 2 * up + core)
    below = (cells, 2 * down + core)
    above_mate = (cells, 2 * up + 1 - core)
    below_mate = (cells, 2 * down + 1 - core)
    snap_of = [lax.rem(snaps + d, 8) for d in (4, 5, 3, 2, 6, 1, 7)]
    snap_peers = [(cells, s) for s in snap_of]
    g_of = [lax.rem(g + d, ng) for d in sorted(range(1, ng), key=lambda d: -min(d, ng - d))]
    g_peers = [((2 * u + lax.rem(o, 2)) * NX + lax.div(o, 2), snaps) for o in g_of]

    def at_u(d):
        return ((2 * lax.rem(u + d, nu) + odd) * NX + x, snaps)

    u_peers = [at_u(d) for d in sorted(range(1, nu), key=lambda d: -min(d, nu - d))]

    def remote(src, dst, ss, rs, to):
        return pltpu.make_async_remote_copy(
            src_ref=src, dst_ref=dst, send_sem=ss, recv_sem=rs,
            device_id=to, device_id_type=MESH,
        )

    def signal(sem, to):
        pl.semaphore_signal(sem, inc=1, device_id=to, device_id_type=MESH)

    chunk_of = []
    for o in (far, up, down, y):
        chunk_of += [(1 - core) * 4 + o, core * 4 + o]
    w_load = pltpu.make_async_copy(w_ref, w_buf, load_sem.at[8])
    w_load.start()
    loads = []
    for i, q in enumerate(chunk_of):
        start = pl.multiple_of(q * ch, ch)
        loads.append(
            pltpu.make_async_copy(a_ref.at[pl.ds(start, ch), :], a_buf.at[i], load_sem.at[i])
        )
    ahead = 2
    for load in loads[:ahead]:
        load.start()

    barrier = pltpu.get_barrier_semaphore()
    near = [mate, above, below]
    near += [(z * NX + lax.rem(x + d, NX), snaps) for d in sorted({1, NX - 1}) if d % NX]
    near += [(lax.rem(z + d, nz) * NX + x, snaps) for d in sorted({1, nz - 1})]
    for peer in near:
        signal(barrier, peer)

    w_load.wait()
    w_h, w_m, w_l = thirds(w_buf[...])
    w_cat = jnp.concatenate([w_h, w_m, w_l], axis=0)

    def sketch_chunk(i):
        loads[i].wait()
        for load in loads[ahead + 2 * i : ahead + 2 * i + 2]:
            load.start()
        h, m, low = thirds(a_buf[i])
        a_h[i], a_m[i], a_l[i] = h, m, low
        return six(w_cat, h, m, low, True)

    swaps = []

    def swap(j):
        swaps.append(remote(send_a.at[j], got_a.at[j], s_a.at[j], r_a.at[j], mate))
        swaps[-1].start()

    rounds = [near, near]
    reach = 1
    while reach < nu // 2:
        rounds.append([at_u(reach), at_u(nu - reach)])
        reach *= 2

    def tell(i):
        for peer in rounds[i] if i < len(rounds) else ():
            signal(know_sem.at[i], peer)

    def hear(i):
        if i < len(rounds):
            pl.semaphore_wait(know_sem.at[i], len(rounds[i]))

    send_a[0] = sketch_chunk(0)
    pl.semaphore_wait(barrier, len(near))
    swap(0)
    far_part = sketch_chunk(1)
    send_a[1] = sketch_chunk(2)
    swap(1)
    tell(0)
    swaps[0].wait_recv()
    rs_a[...] = far_part + got_a[0]
    b_up = remote(rs_a.at[0:16], rs_b.at[0], s_b.at[0], r_b.at[0], above)
    b_up.start()
    b_down = remote(rs_a.at[16:32], rs_b.at[1], s_b.at[1], r_b.at[1], below)
    b_down.start()
    up_part = sketch_chunk(3)
    send_a[2] = sketch_chunk(4)
    swap(2)
    hear(0)
    tell(1)
    down_part = sketch_chunk(5)
    swaps[1].wait_recv()
    up_part = up_part + got_a[1]
    rs_c[0, 16:32] = up_part[16:32]
    c_up = [remote(rs_c.at[0, 16:32], rs_d.at[0, 16:32], s_c.at[0], r_c.at[0], above)]
    c_up[0].start()
    send_a[3] = sketch_chunk(6)
    swap(3)
    swaps[2].wait_recv()
    down_part = down_part + got_a[2]
    rs_c[1, 0:16] = down_part[0:16]
    c_down = [remote(rs_c.at[1, 0:16], rs_d.at[1, 0:16], s_c.at[1], r_c.at[1], below)]
    c_down[0].start()
    own_part = sketch_chunk(7)
    hear(1)
    tell(2)
    b_up.wait_recv()
    rs_c[0, 0:16] = up_part[0:16] + rs_b[0]
    c_up.append(remote(rs_c.at[0, 0:16], rs_d.at[0, 0:16], s_c.at[2], r_c.at[2], above))
    c_up[1].start()
    b_down.wait_recv()
    rs_c[1, 16:32] = down_part[16:32] + rs_b[1]
    c_down.append(remote(rs_c.at[1, 16:32], rs_d.at[1, 16:32], s_c.at[3], r_c.at[3], below))
    c_down[1].start()
    swaps[3].wait_recv()
    own_part = own_part + got_a[3]
    hear(2)
    tell(3)
    for copy in c_up + c_down:
        copy.wait_recv()
    own = core * 4 + y
    own_rows = own_part + rs_d[0] + rs_d[1]
    s_all[own] = own_rows

    first, second = pl.ds(0, 16), pl.ds(16, 16)

    def along(slot, rows, sem, to, s, r):
        piece = s_all.at[slot, rows]
        return remote(piece, piece, s.at[sem], r.at[sem], to)

    gathers = [
        along(own, first, 0, above, s_y, r_y),
        along(own, second, 1, below, s_y, r_y),
        along(own, second, 2, above, s_y, r_y),
        along(own, first, 3, below, s_y, r_y),
    ]
    for copy in gathers:
        copy.start()

    passes = []

    def pass_on(slot):
        sem = len(passes)
        copy = remote(s_all.at[slot], s_all.at[slot], s_p.at[sem], r_p.at[sem], mate)
        copy.start()
        passes.append(copy)

    pass_on(own)

    gram_h, gram_l = packed_gram(own_rows)
    for r in range(8):
        go[r, 0] = gram_h[r : r + 1]
        go[r, 1] = gram_l[r : r + 1]

    def quarter_of(s):
        return 2 * lax.rem(s, 2) + lax.rem(lax.div(s, 2), 2)

    quarter = quarter_of(snaps)
    for r in range(2):
        gs[snaps, r] = go[2 * quarter + r]
    for s, peer in zip(snap_of, snap_peers):
        piece = go.at[pl.ds(2 * quarter_of(s), 2)]
        remote(piece, gs.at[snaps], s_m.at[0], r_m.at[0], peer).start()

    def whole(buf, count, sem):
        piece = buf.at[pl.ds(0, count)]
        return remote(piece, piece, s_m.at[sem], r_m.at[sem], mate)

    def pair_sum(buf, count):
        return sum_pairs([(buf[i, :, 0], buf[i, :, 1]) for i in range(count)])

    def row_sum(buf, count):
        rows = [buf[i] for i in range(count)]
        while len(rows) > 1:
            rows = [rows[i] + rows[i + 1] for i in range(0, len(rows), 2)]
        return rows[0]

    def projected(i, slot):
        s_h, s_m, s_l = thirds(s_all[slot])
        s_cat[slot, 0:n] = s_h
        s_cat[slot, n : 2 * n] = s_m
        s_cat[slot, 2 * n : 3 * n] = s_l
        s_cat[slot, 3 * n : 4 * n] = s_h
        s_cat[slot, 4 * n : 5 * n] = s_m
        s_cat[slot, 5 * n : 6 * n] = s_h
        lhs = jnp.concatenate([s_h, s_m, s_l], axis=0)
        return six(lhs, a_h[i], a_m[i], a_l[i], False)

    theirs = (1 - core) * 4
    slot_down, slot_up, slot_far = core * 4 + down, core * 4 + up, core * 4 + far
    w_sum = projected(7, own)
    passes[0].wait_recv()
    w_sum += projected(6, theirs + y)
    along(slot_down, first, 0, above, s_y, r_y).wait_recv()
    forwards = [along(slot_down, first, 0, above, s_f, r_f)]
    forwards[0].start()
    along(slot_up, second, 1, below, s_y, r_y).wait_recv()
    forwards.append(along(slot_up, second, 1, below, s_f, r_f))
    forwards[1].start()
    forwards.append(along(slot_down, first, 2, above_mate, s_f, r_f))
    forwards[2].start()
    forwards.append(along(slot_up, second, 3, below_mate, s_f, r_f))
    forwards[3].start()
    along(slot_down, second, 2, above, s_y, r_y).wait_recv()
    pass_on(slot_down)
    along(slot_up, first, 3, below, s_y, r_y).wait_recv()
    pass_on(slot_up)

    gs_done = whole(gs, 7, 0)
    gs_done.wait_recv()
    hi, lo = pair_sum(gs, 8)
    gx[g, :, 0], gx[g, :, 1] = hi, lo
    for peer in g_peers:
        remote(gx.at[g], gx.at[g], s_m.at[1], r_m.at[1], peer).start()

    w_sum += projected(5, slot_down)
    w_sum += projected(3, slot_up)
    forwards[0].wait_recv()
    forwards[1].wait_recv()
    passes[1].wait_recv()
    w_sum += projected(4, theirs + down)
    passes[2].wait_recv()
    w_sum += projected(2, theirs + up)
    w_sum += projected(1, slot_far)

    hear(3)
    gx_done = whole(gx, ng - 1, 1)
    gx_done.wait_recv()
    hi, lo = pair_sum(gx, ng)
    gz[u, :, 0], gz[u, :, 1] = hi, lo
    for peer in u_peers:
        remote(gz.at[u], gz.at[u], s_m.at[3], r_m.at[3], peer).start()

    forwards[2].wait_recv()
    forwards[3].wait_recv()
    w_sum += projected(0, theirs + far)

    share = n // ng
    for i in range(ng):
        wp[i] = w_sum[i * share : (i + 1) * share]
    wx[g] = wp[g]
    for o, peer in zip(g_of, g_peers):
        remote(wp.at[o], wx.at[g], s_m.at[2], r_m.at[2], peer).start()

    wx_done = whole(wx, ng - 1, 2)
    wx_done.wait_recv()
    wz[u] = row_sum(wx, ng)
    for peer in u_peers:
        remote(wz.at[u], wz.at[u], s_m.at[4], r_m.at[4], peer).start()

    gz_done = whole(gz, nu - 1, 3)
    gz_done.wait_recv()
    hi, lo = pair_sum(gz, nu)
    ga[quarter, :, 0], ga[quarter, :, 1] = hi, lo
    twin = 4 * lax.div(y, 2) + 2 - 2 * lax.rem(y, 2)
    for peer in ((cells, twin + core), (cells, twin + 1 - core), mate):
        remote(ga.at[quarter], ga.at[quarter], s_m.at[5], r_m.at[5], peer).start()
    ga_done = whole(ga, 3, 5)
    ga_done.wait_recv()

    for r in range(8):
        gt[0, r : r + 1, :] = ga[r // 2, r % 2, 0]
        gt[1, r : r + 1, :] = ga[r // 2, r % 2, 1]
    lane8 = lax.broadcasted_iota(jnp.int32, (8, 128), 1)
    sub8 = lax.broadcasted_iota(jnp.int32, (8, 128), 0)
    tiles_h, tiles_l = [], []
    for i in range(4):
        eye = jnp.where(lane8 - n == sub8 + 8 * i, 1.0, 0.0)
        turned_h = gt[0] if i == 0 else pltpu.roll(gt[0], 128 - n * i, 1)
        turned_l = gt[1] if i == 0 else pltpu.roll(gt[1], 128 - n * i, 1)
        tiles_h.append(jnp.where(lane8 < n, turned_h, eye))
        tiles_l.append(jnp.where(lane8 < n, turned_l, 0.0))
    wz_done = whole(wz, nu - 1, 4)

    def share_w():
        wz_done.wait_recv()
        wa[g] = row_sum(wz, nu)
        for peer in g_peers:
            remote(wa.at[g], wa.at[g], s_m.at[6], r_m.at[6], peer).start()

    factor = jnp.concatenate(eliminate(tiles_h, tiles_l, share_w), axis=0)

    f_h, f_m, f_l = thirds(factor)
    f_h, f_m, f_l = f_h.astype(F32), f_m.astype(F32), f_l.astype(F32)
    which = lax.broadcasted_iota(jnp.int32, (n, 128), 1) // n
    left = jnp.where(
        which == 0, pltpu.roll(f_h, 96, 1),
        jnp.where(which == 1, f_h, jnp.where(which == 2, pltpu.roll(f_h, 32, 1), pltpu.roll(f_m, 64, 1))),
    )
    right = jnp.where(which == 0, pltpu.roll(f_m, 96, 1), f_l)
    inv_cat = jnp.concatenate([left, right[:, : 2 * n]], axis=1).astype(BF16)
    root = math.sqrt(total_cells)
    writes = []
    for q in range(8):
        columns = slice(q * ch, (q + 1) * ch)
        out_b[:, columns] = dot(inv_cat, s_cat[q]) * root
        writes.append(
            pltpu.make_async_copy(out_b.at[:, columns], basis_ref.at[:, columns], out_sem.at[q])
        )
        writes[-1].start()

    wa_done = whole(wa, ng - 1, 6)
    wa_done.wait_recv()
    w_total = jnp.concatenate([wa[i] for i in range(ng)], axis=0)
    t_h, t_m, t_l = thirds(w_total)
    out_c[...] = dot(inv_cat, jnp.concatenate([t_h, t_m, t_l, t_h, t_m, t_h], axis=0))
    writes.append(pltpu.make_async_copy(out_c, coef_ref, out_sem.at[8]))
    writes[-1].start()

    for copy in swaps + [b_up, b_down] + c_up + c_down + gathers + forwards + passes:
        copy.wait_send()
    for copy in (gs_done, gx_done, wx_done, gz_done, wz_done, ga_done, wa_done):
        copy.wait_send()
    for copy in writes:
        copy.wait()


def deliver(*arrays):
    count = len(arrays)
    pieces = [(i, r) for i, a in enumerate(arrays) for r in range(0, a.shape[0], 8)]

    def body(*refs):
        copies = []
        for sem, (i, r) in enumerate(pieces):
            rows = pl.ds(r, 8)
            copies.append(
                pltpu.make_async_copy(
                    refs[i].at[rows, :], refs[count + i].at[rows, :], refs[-1].at[sem]
                )
            )
        for copy in copies:
            copy.start()
        for copy in copies:
            copy.wait()

    return pl.pallas_call(
        body,
        out_shape=tuple(jax.ShapeDtypeStruct(a.shape, a.dtype) for a in arrays),
        in_specs=[pl.BlockSpec(memory_space=pl.ANY)] * count,
        out_specs=(pl.BlockSpec(memory_space=pl.ANY),) * count,
        scratch_shapes=[pltpu.SemaphoreType.DMA((len(pieces),))],
        compiler_params=pltpu.CompilerParams(vmem_limit_bytes=1 << 20),
    )(*arrays)


def shards(snapshots, sketch):
    cells, snaps = snapshots.shape
    n = sketch.shape[1]
    nz = lax.axis_size("cells") // NX
    ch = cells // 8
    total = cells * lax.axis_size("cells")
    share = n // (2 * NX)
    dma = pltpu.SemaphoreType.DMA
    vm = pltpu.VMEM
    basis, coefficients = pl.pallas_call(
        functools.partial(kernel, nz, ch, total),
        out_shape=(
            jax.ShapeDtypeStruct((n, cells), F32),
            jax.ShapeDtypeStruct((n, snaps), F32),
        ),
        in_specs=[
            pl.BlockSpec(memory_space=pltpu.HBM),
            pl.BlockSpec(memory_space=pltpu.HBM),
        ],
        out_specs=(
            pl.BlockSpec(memory_space=pl.ANY),
            pl.BlockSpec(memory_space=pl.ANY),
        ),
        scratch_shapes=[
            vm((n, snaps), F32), vm((8, ch, snaps), F32),
            vm((8, ch, snaps), BF16), vm((8, ch, snaps), BF16), vm((8, ch, snaps), BF16),
            vm((4, n, ch), F32), vm((4, n, ch), F32),
            vm((n, ch), F32), vm((2, n // 2, ch), F32),
            vm((2, n, ch), F32), vm((2, n, ch), F32),
            vm((8, n, ch), F32), vm((8, 6 * n, ch), BF16),
            vm((8, 2, 1, 128), F32), vm((8, 2, 2, 1, 128), F32),
            vm((2 * NX, 2, 2, 1, 128), F32), vm((nz // 2, 2, 2, 1, 128), F32),
            vm((4, 2, 2, 1, 128), F32), vm((2, 8, 128), F32),
            vm((2 * NX, share, snaps), F32), vm((2 * NX, share, snaps), F32),
            vm((nz // 2, share, snaps), F32), vm((2 * NX, share, snaps), F32),
            vm((n, cells), F32), vm((n, snaps), F32),
            dma((9,)), dma((4,)), dma((4,)), dma((2,)), dma((2,)), dma((4,)), dma((4,)),
            dma((4,)), dma((4,)), dma((4,)), dma((4,)), dma((3,)), dma((3,)),
            dma((7,)), dma((7,)), dma((9,)), pltpu.SemaphoreType.REGULAR((4,)),
        ],
        compiler_params=pltpu.CompilerParams(
            collective_id=0, has_side_effects=True, vmem_limit_bytes=52 << 20
        ),
    )(snapshots, jnp.transpose(sketch))
    return deliver(basis, coefficients)


def solution(mesh):
    return jax.shard_map(
        shards,
        mesh=mesh,
        in_specs=(P("cells", "snaps"), P("snaps", None)),
        out_specs=(P(None, "cells"), P(None, "snaps")),
        check_vma=False,
    )
```

```python
import functools
import math

import jax
import jax.numpy as jnp
from jax import lax
from jax.experimental import pallas as pl
from jax.experimental.pallas import tpu as pltpu
from jax.sharding import PartitionSpec as P

MESH = pl.DeviceIdType.MESH
NX = 4
F32 = jnp.float32
BF16 = jnp.bfloat16
ROWS = 32


def two_sum(a, b):
    s = a + b
    t = s - a
    return s, (a - (s - t)) + (b - t)


def quick_two_sum(a, b):
    s = a + b
    return s, b - (s - a)


def halves(a):
    c = a * 4097.0
    high = c - (c - a)
    return high, a - high


def two_prod(a, ah, al, b, bh, bl):
    p = a * b
    return p, ((ah * bh - p) + ah * bl + al * bh) + al * bl


def dd_add(ah, al, bh, bl):
    s, e = two_sum(ah, bh)
    return quick_two_sum(s, e + (al + bl))


def thirds(a):
    h = a.astype(BF16)
    rest = a - h.astype(F32)
    m = rest.astype(BF16)
    low = (rest - m.astype(F32)).astype(BF16)
    return h, m, low


def dot(a, b, transposed=False):
    dims = (((1,), (1 if transposed else 0,)), ((), ()))
    return lax.dot_general(a, b, dims, preferred_element_type=F32)


def six(lhs, h, m, low, transposed):
    n = ROWS
    dh = dot(lhs, h, transposed)
    dm = dot(lhs[: 2 * n], m, transposed)
    dl = dot(lhs[:n], low, transposed)
    small = (dh[2 * n :] + dm[n:]) + dl
    return dh[:n] + ((dh[n : 2 * n] + dm[:n]) + small)


def sum_pairs(pairs):
    while len(pairs) > 1:
        pairs = [
            dd_add(*pairs[i], *pairs[i + 1]) if i + 1 < len(pairs) else pairs[i]
            for i in range(0, len(pairs), 2)
        ]
    return pairs[0]


def power_above(x):
    p = jnp.full(x.shape, 2.0**-63, F32)
    inverse = jnp.full(x.shape, 2.0**63, F32)
    for step in (64, 32, 16, 8, 4, 2, 1):
        larger = x >= p * (2.0**step)
        p = jnp.where(larger, p * (2.0**step), p)
        inverse = jnp.where(larger, inverse * (2.0**-step), inverse)
    return p * 2.0, inverse * 0.5


def eliminate(gh, gl, midway=None, block=4):
    gh, gl = list(gh), list(gl)
    tiles = len(gh)
    last = 8 * tiles - 1
    sub = lax.broadcasted_iota(jnp.int32, (8, 128), 0)
    lane = lax.broadcasted_iota(jnp.int32, (8, 128), 1)

    def across(tile, k):
        return jnp.broadcast_to(tile[:, k : k + 1], (8, 128))

    def down(tile, r):
        return jnp.broadcast_to(tile[r : r + 1, :], (8, 128))

    for start in range(0, last, block):
        if midway is not None and start == 16:
            midway()
        ib = start // 8
        columns = [
            {t: (across(gh[t], k), across(gl[t], k)) for t in range(ib, tiles)}
            for k in range(start, start + block)
        ]
        for j in range(block):
            k, kr = start + j, (start + j) % 8
            if k == last:
                break
            ph, plo = (down(v, kr) for v in columns[j][ib])
            r = 1.0 / ph
            ra, rb = halves(r)

            def scaled(h, low):
                ha, hb = halves(h)
                p, e = two_prod(h, ha, hb, r, ra, rb)
                return p, e + low * r

            one, rest = scaled(ph, plo)
            slip = (one - 1.0) + rest
            uh, ul = scaled(down(gh[ib], kr), down(gl[ib], kr))
            rows = [(uh, ul) + halves(uh)]
            for i in range(j + 1, block):
                vh, vl = scaled(*(down(v, kr) for v in columns[i][ib]))
                rows.append((vh, vl) + halves(vh))
            for t in range(ib if kr < 7 else ib + 1, tiles):
                ch, cl = columns[j][t]
                slip_t = slip
                if t == ib:
                    ch = jnp.where(sub > kr, ch, 0.0)
                    cl = jnp.where(sub > kr, cl, 0.0)
                    slip_t = jnp.where(sub > kr, slip, 0.0)
                ca, cb = halves(ch)

                def reduced(h, low, row):
                    vh, vl, va, vb = row
                    p, e = two_prod(ch, ca, cb, vh, va, vb)
                    e = (ch * vl + cl * vh) + e
                    s, d = two_sum(h, -p)
                    return quick_two_sum(s, d + ((low + h * slip_t) - e))

                gh[t], gl[t] = reduced(gh[t], gl[t], rows[0])
                for i in range(j + 1, block):
                    columns[i][t] = reduced(*columns[i][t], rows[i - j])
    out = []
    for t in range(tiles):
        at = lane == sub + 8 * t
        d = jnp.sum(jnp.where(at, gh[t], 0.0), axis=1, keepdims=True)
        y = lax.rsqrt(d)
        y = y * (1.5 - 0.5 * d * y * y)
        out.append((gh[t] + gl[t]) * y)
    return out


def packed_gram(rows):
    n = ROWS
    top = jnp.max(jnp.abs(rows), axis=1, keepdims=True)
    scale, inverse = power_above(jnp.broadcast_to(top, (n, 128)))
    v = rows * (inverse[:, 0:1] * 64.0)
    parts = []
    for a in range(4):
        whole = jnp.round(v)
        parts.append(whole.astype(BF16))
        v = (v - whole) * 128.0
    slices = jnp.concatenate(parts, axis=0)
    products = dot(slices, slices, True)
    wide = lax.broadcasted_iota(jnp.int32, (n, 128), 1)
    tall = lax.broadcasted_iota(jnp.int32, (n, 128), 0)
    group = wide // n
    weight = jnp.where(
        group == 0, 2.0**-12,
        jnp.where(group == 1, 2.0**-19, jnp.where(group == 2, 2.0**-26, 2.0**-33)),
    )
    gh, gl = two_sum(products[0:n] * weight, products[n : 2 * n] * (weight * 2.0**-7))
    for a in (2, 3):
        gh, gl = dd_add(gh, gl, products[a * n : (a + 1) * n] * (weight * 2.0 ** (-7 * a)), 0.0)
    for turn in (64, 32):
        gh, gl = dd_add(gh, gl, pltpu.roll(gh, turn, 1), pltpu.roll(gl, turn, 1))
    column_scale = jnp.sum(jnp.where(wide - n * group == tall, scale, 0.0), axis=0, keepdims=True)
    both = scale * column_scale
    gh, gl = gh * both, gl * both
    lanes = lax.broadcasted_iota(jnp.int32, (8, 128), 1) // n

    def pack(g):
        out = g[0:8]
        for i in range(1, 4):
            out = jnp.where(lanes == i, g[8 * i : 8 * i + 8], out)
        return out

    return pack(gh), pack(gl)


def kernel(
    nz, ch, total_cells,
    a_ref, w_ref, basis_ref, coef_ref,
    w_buf, a_buf, a_h, a_m, a_l,
    send_a, got_a, rs_a, rs_b, rs_c, rs_d, s_all, s_cat,
    go, gs, gx, gz, ga, gt,
    wp, wx, wz, wa, out_b, out_c,
    load_sem, s_a, r_a, s_b, r_b, s_c, r_c, s_y, r_y, s_f, r_f, s_p, r_p, s_m, r_m,
    out_sem, know_sem,
):
    cells = lax.axis_index("cells")
    snaps = lax.axis_index("snaps")
    n = ROWS
    ng, nu = 2 * NX, nz // 2
    z, x = lax.div(cells, NX), lax.rem(cells, NX)
    u, odd = lax.div(z, 2), lax.rem(z, 2)
    y, core = lax.div(snaps, 2), lax.rem(snaps, 2)
    g = 2 * x + odd
    up, down, far = lax.rem(y + 1, 4), lax.rem(y + 3, 4), lax.rem(y + 2, 4)
    mate = (cells, 2 * y + 1 - core)
    above = (cells, 2 * up + core)
    below = (cells, 2 * down + core)
    above_mate = (cells, 2 * up + 1 - core)
    below_mate = (cells, 2 * down + 1 - core)
    snap_of = [lax.rem(snaps + d, 8) for d in (4, 5, 3, 2, 6, 1, 7)]
    snap_peers = [(cells, s) for s in snap_of]
    g_of = [lax.rem(g + d, ng) for d in sorted(range(1, ng), key=lambda d: -min(d, ng - d))]
    g_peers = [((2 * u + lax.rem(o, 2)) * NX + lax.div(o, 2), snaps) for o in g_of]

    def at_u(d):
        return ((2 * lax.rem(u + d, nu) + odd) * NX + x, snaps)

    u_peers = [at_u(d) for d in sorted(range(1, nu), key=lambda d: -min(d, nu - d))]

    def remote(src, dst, ss, rs, to):
        return pltpu.make_async_remote_copy(
            src_ref=src, dst_ref=dst, send_sem=ss, recv_sem=rs,
            device_id=to, device_id_type=MESH,
        )

    def signal(sem, to):
        pl.semaphore_signal(sem, inc=1, device_id=to, device_id_type=MESH)

    chunk_of = []
    for o in (far, up, down, y):
        chunk_of += [(1 - core) * 4 + o, core * 4 + o]
    w_load = pltpu.make_async_copy(w_ref, w_buf, load_sem.at[8])
    w_load.start()
    loads = []
    for i, q in enumerate(chunk_of):
        start = pl.multiple_of(q * ch, ch)
        loads.append(
            pltpu.make_async_copy(a_ref.at[pl.ds(start, ch), :], a_buf.at[i], load_sem.at[i])
        )
    ahead = 2
    for load in loads[:ahead]:
        load.start()

    barrier = pltpu.get_barrier_semaphore()
    near = [mate, above, below]
    near += [(z * NX + lax.rem(x + d, NX), snaps) for d in sorted({1, NX - 1}) if d % NX]
    near += [(lax.rem(z + d, nz) * NX + x, snaps) for d in sorted({1, nz - 1})]
    for peer in near:
        signal(barrier, peer)

    w_load.wait()
    w_h, w_m, w_l = thirds(w_buf[...])
    w_cat = jnp.concatenate([w_h, w_m, w_l], axis=0)

    def sketch_chunk(i):
        loads[i].wait()
        for load in loads[ahead + 2 * i : ahead + 2 * i + 2]:
            load.start()
        h, m, low = thirds(a_buf[i])
        a_h[i], a_m[i], a_l[i] = h, m, low
        return six(w_cat, h, m, low, True)

    swaps = []

    def swap(j):
        swaps.append(remote(send_a.at[j], got_a.at[j], s_a.at[j], r_a.at[j], mate))
        swaps[-1].start()

    rounds = [near, near]
    reach = 1
    while reach < nu // 2:
        rounds.append([at_u(reach), at_u(nu - reach)])
        reach *= 2

    def tell(i):
        for peer in rounds[i] if i < len(rounds) else ():
            signal(know_sem.at[i], peer)

    def hear(i):
        if i < len(rounds):
            pl.semaphore_wait(know_sem.at[i], len(rounds[i]))

    send_a[0] = sketch_chunk(0)
    pl.semaphore_wait(barrier, len(near))
    swap(0)
    far_part = sketch_chunk(1)
    send_a[1] = sketch_chunk(2)
    swap(1)
    tell(0)
    swaps[0].wait_recv()
    rs_a[...] = far_part + got_a[0]
    b_up = remote(rs_a.at[0:16], rs_b.at[0], s_b.at[0], r_b.at[0], above)
    b_up.start()
    b_down = remote(rs_a.at[16:32], rs_b.at[1], s_b.at[1], r_b.at[1], below)
    b_down.start()
    up_part = sketch_chunk(3)
    send_a[2] = sketch_chunk(4)
    swap(2)
    hear(0)
    tell(1)
    down_part = sketch_chunk(5)
    swaps[1].wait_recv()
    up_part = up_part + got_a[1]
    rs_c[0, 16:32] = up_part[16:32]
    c_up = [remote(rs_c.at[0, 16:32], rs_d.at[0, 16:32], s_c.at[0], r_c.at[0], above)]
    c_up[0].start()
    send_a[3] = sketch_chunk(6)
    swap(3)
    swaps[2].wait_recv()
    down_part = down_part + got_a[2]
    rs_c[1, 0:16] = down_part[0:16]
    c_down = [remote(rs_c.at[1, 0:16], rs_d.at[1, 0:16], s_c.at[1], r_c.at[1], below)]
    c_down[0].start()
    own_part = sketch_chunk(7)
    hear(1)
    tell(2)
    b_up.wait_recv()
    rs_c[0, 0:16] = up_part[0:16] + rs_b[0]
    c_up.append(remote(rs_c.at[0, 0:16], rs_d.at[0, 0:16], s_c.at[2], r_c.at[2], above))
    c_up[1].start()
    b_down.wait_recv()
    rs_c[1, 16:32] = down_part[16:32] + rs_b[1]
    c_down.append(remote(rs_c.at[1, 16:32], rs_d.at[1, 16:32], s_c.at[3], r_c.at[3], below))
    c_down[1].start()
    swaps[3].wait_recv()
    own_part = own_part + got_a[3]
    hear(2)
    tell(3)
    for copy in c_up + c_down:
        copy.wait_recv()
    own = core * 4 + y
    own_rows = own_part + rs_d[0] + rs_d[1]
    s_all[own] = own_rows

    first, second = pl.ds(0, 16), pl.ds(16, 16)

    def along(slot, rows, sem, to, s, r):
        piece = s_all.at[slot, rows]
        return remote(piece, piece, s.at[sem], r.at[sem], to)

    gathers = [
        along(own, first, 0, above, s_y, r_y),
        along(own, second, 1, below, s_y, r_y),
        along(own, second, 2, above, s_y, r_y),
        along(own, first, 3, below, s_y, r_y),
    ]
    for copy in gathers:
        copy.start()

    passes = []

    def pass_on(slot):
        sem = len(passes)
        copy = remote(s_all.at[slot], s_all.at[slot], s_p.at[sem], r_p.at[sem], mate)
        copy.start()
        passes.append(copy)

    pass_on(own)

    gram_h, gram_l = packed_gram(own_rows)
    for r in range(8):
        go[r, 0] = gram_h[r : r + 1]
        go[r, 1] = gram_l[r : r + 1]

    def quarter_of(s):
        return 2 * lax.rem(s, 2) + lax.rem(lax.div(s, 2), 2)

    quarter = quarter_of(snaps)
    for r in range(2):
        gs[snaps, r] = go[2 * quarter + r]
    for s, peer in zip(snap_of, snap_peers):
        piece = go.at[pl.ds(2 * quarter_of(s), 2)]
        remote(piece, gs.at[snaps], s_m.at[0], r_m.at[0], peer).start()

    def whole(buf, count, sem):
        piece = buf.at[pl.ds(0, count)]
        return remote(piece, piece, s_m.at[sem], r_m.at[sem], mate)

    def pair_sum(buf, count):
        return sum_pairs([(buf[i, :, 0], buf[i, :, 1]) for i in range(count)])

    def row_sum(buf, count):
        rows = [buf[i] for i in range(count)]
        while len(rows) > 1:
            rows = [rows[i] + rows[i + 1] for i in range(0, len(rows), 2)]
        return rows[0]

    def projected(i, slot):
        s_h, s_m, s_l = thirds(s_all[slot])
        s_cat[slot, 0:n] = s_h
        s_cat[slot, n : 2 * n] = s_m
        s_cat[slot, 2 * n : 3 * n] = s_l
        s_cat[slot, 3 * n : 4 * n] = s_h
        s_cat[slot, 4 * n : 5 * n] = s_m
        s_cat[slot, 5 * n : 6 * n] = s_h
        lhs = jnp.concatenate([s_h, s_m, s_l], axis=0)
        return six(lhs, a_h[i], a_m[i], a_l[i], False)

    theirs = (1 - core) * 4
    slot_down, slot_up, slot_far = core * 4 + down, core * 4 + up, core * 4 + far
    w_sum = projected(7, own)
    passes[0].wait_recv()
    w_sum += projected(6, theirs + y)
    along(slot_down, first, 0, above, s_y, r_y).wait_recv()
    forwards = [along(slot_down, first, 0, above, s_f, r_f)]
    forwards[0].start()
    along(slot_up, second, 1, below, s_y, r_y).wait_recv()
    forwards.append(along(slot_up, second, 1, below, s_f, r_f))
    forwards[1].start()
    forwards.append(along(slot_down, first, 2, above_mate, s_f, r_f))
    forwards[2].start()
    forwards.append(along(slot_up, second, 3, below_mate, s_f, r_f))
    forwards[3].start()
    along(slot_down, second, 2, above, s_y, r_y).wait_recv()
    pass_on(slot_down)
    along(slot_up, first, 3, below, s_y, r_y).wait_recv()
    pass_on(slot_up)

    gs_done = whole(gs, 7, 0)
    gs_done.wait_recv()
    hi, lo = pair_sum(gs, 8)
    gx[g, :, 0], gx[g, :, 1] = hi, lo
    for peer in g_peers:
        remote(gx.at[g], gx.at[g], s_m.at[1], r_m.at[1], peer).start()

    w_sum += projected(5, slot_down)
    w_sum += projected(3, slot_up)
    forwards[0].wait_recv()
    forwards[1].wait_recv()
    passes[1].wait_recv()
    w_sum += projected(4, theirs + down)
    passes[2].wait_recv()
    w_sum += projected(2, theirs + up)
    w_sum += projected(1, slot_far)

    hear(3)
    gx_done = whole(gx, ng - 1, 1)
    gx_done.wait_recv()
    hi, lo = pair_sum(gx, ng)
    gz[u, :, 0], gz[u, :, 1] = hi, lo
    for peer in u_peers:
        remote(gz.at[u], gz.at[u], s_m.at[3], r_m.at[3], peer).start()

    forwards[2].wait_recv()
    forwards[3].wait_recv()
    w_sum += projected(0, theirs + far)

    share = n // ng
    for i in range(ng):
        wp[i] = w_sum[i * share : (i + 1) * share]
    wx[g] = wp[g]
    for o, peer in zip(g_of, g_peers):
        remote(wp.at[o], wx.at[g], s_m.at[2], r_m.at[2], peer).start()

    wx_done = whole(wx, ng - 1, 2)
    wx_done.wait_recv()
    wz[u] = row_sum(wx, ng)
    for peer in u_peers:
        remote(wz.at[u], wz.at[u], s_m.at[4], r_m.at[4], peer).start()

    gz_done = whole(gz, nu - 1, 3)
    gz_done.wait_recv()
    hi, lo = pair_sum(gz, nu)
    ga[quarter, :, 0], ga[quarter, :, 1] = hi, lo
    twin = 4 * lax.div(y, 2) + 2 - 2 * lax.rem(y, 2)
    for peer in ((cells, twin + core), (cells, twin + 1 - core), mate):
        remote(ga.at[quarter], ga.at[quarter], s_m.at[5], r_m.at[5], peer).start()
    ga_done = whole(ga, 3, 5)
    ga_done.wait_recv()

    for r in range(8):
        gt[0, r : r + 1, :] = ga[r // 2, r % 2, 0]
        gt[1, r : r + 1, :] = ga[r // 2, r % 2, 1]
    lane8 = lax.broadcasted_iota(jnp.int32, (8, 128), 1)
    sub8 = lax.broadcasted_iota(jnp.int32, (8, 128), 0)
    tiles_h, tiles_l = [], []
    for i in range(4):
        eye = jnp.where(lane8 - n == sub8 + 8 * i, 1.0, 0.0)
        turned_h = gt[0] if i == 0 else pltpu.roll(gt[0], 128 - n * i, 1)
        turned_l = gt[1] if i == 0 else pltpu.roll(gt[1], 128 - n * i, 1)
        tiles_h.append(jnp.where(lane8 < n, turned_h, eye))
        tiles_l.append(jnp.where(lane8 < n, turned_l, 0.0))
    wz_done = whole(wz, nu - 1, 4)

    def share_w():
        wz_done.wait_recv()
        wa[g] = row_sum(wz, nu)
        for peer in g_peers:
            remote(wa.at[g], wa.at[g], s_m.at[6], r_m.at[6], peer).start()

    factor = jnp.concatenate(eliminate(tiles_h, tiles_l, share_w), axis=0)

    f_h, f_m, f_l = thirds(factor)
    f_h, f_m, f_l = f_h.astype(F32), f_m.astype(F32), f_l.astype(F32)
    which = lax.broadcasted_iota(jnp.int32, (n, 128), 1) // n
    left = jnp.where(
        which == 0, pltpu.roll(f_h, 96, 1),
        jnp.where(which == 1, f_h, jnp.where(which == 2, pltpu.roll(f_h, 32, 1), pltpu.roll(f_m, 64, 1))),
    )
    right = jnp.where(which == 0, pltpu.roll(f_m, 96, 1), f_l)
    inv_cat = jnp.concatenate([left, right[:, : 2 * n]], axis=1).astype(BF16)
    root = math.sqrt(total_cells)
    writes = []
    for q in range(8):
        columns = slice(q * ch, (q + 1) * ch)
        out_b[:, columns] = dot(inv_cat, s_cat[q]) * root
        writes.append(
            pltpu.make_async_copy(out_b.at[:, columns], basis_ref.at[:, columns], out_sem.at[q])
        )
        writes[-1].start()

    for copy in swaps + [b_up, b_down] + c_up + c_down + gathers + forwards + passes:
        copy.wait_send()
    for copy in (gs_done, gx_done, wx_done, gz_done, wz_done, ga_done):
        copy.wait_send()
    for copy in writes:
        copy.wait()

    wa_done = whole(wa, ng - 1, 6)
    wa_done.wait_recv()
    w_total = jnp.concatenate([wa[i] for i in range(ng)], axis=0)
    t_h, t_m, t_l = thirds(w_total)
    out_c[...] = dot(inv_cat, jnp.concatenate([t_h, t_m, t_l, t_h, t_m, t_h], axis=0))
    writes.append(pltpu.make_async_copy(out_c, coef_ref, out_sem.at[8]))
    writes[-1].start()

    writes[-1].wait()
    wa_done.wait_send()


def deliver(*arrays):
    count = len(arrays)
    pieces = [(i, r) for i, a in enumerate(arrays) for r in range(0, a.shape[0], 8)]

    def body(*refs):
        copies = []
        for sem, (i, r) in enumerate(pieces):
            rows = pl.ds(r, 8)
            copies.append(
                pltpu.make_async_copy(
                    refs[i].at[rows, :], refs[count + i].at[rows, :], refs[-1].at[sem]
                )
            )
        for copy in copies:
            copy.start()
        for copy in copies:
            copy.wait()

    return pl.pallas_call(
        body,
        out_shape=tuple(jax.ShapeDtypeStruct(a.shape, a.dtype) for a in arrays),
        in_specs=[pl.BlockSpec(memory_space=pl.ANY)] * count,
        out_specs=(pl.BlockSpec(memory_space=pl.ANY),) * count,
        scratch_shapes=[pltpu.SemaphoreType.DMA((len(pieces),))],
        compiler_params=pltpu.CompilerParams(vmem_limit_bytes=1 << 20),
    )(*arrays)


def shards(snapshots, sketch):
    cells, snaps = snapshots.shape
    n = sketch.shape[1]
    nz = lax.axis_size("cells") // NX
    ch = cells // 8
    total = cells * lax.axis_size("cells")
    share = n // (2 * NX)
    dma = pltpu.SemaphoreType.DMA
    vm = pltpu.VMEM
    basis, coefficients = pl.pallas_call(
        functools.partial(kernel, nz, ch, total),
        out_shape=(
            jax.ShapeDtypeStruct((n, cells), F32),
            jax.ShapeDtypeStruct((n, snaps), F32),
        ),
        in_specs=[
            pl.BlockSpec(memory_space=pltpu.HBM),
            pl.BlockSpec(memory_space=pltpu.HBM),
        ],
        out_specs=(
            pl.BlockSpec(memory_space=pl.ANY),
            pl.BlockSpec(memory_space=pl.ANY),
        ),
        scratch_shapes=[
            vm((n, snaps), F32), vm((8, ch, snaps), F32),
            vm((8, ch, snaps), BF16), vm((8, ch, snaps), BF16), vm((8, ch, snaps), BF16),
            vm((4, n, ch), F32), vm((4, n, ch), F32),
            vm((n, ch), F32), vm((2, n // 2, ch), F32),
            vm((2, n, ch), F32), vm((2, n, ch), F32),
            vm((8, n, ch), F32), vm((8, 6 * n, ch), BF16),
            vm((8, 2, 1, 128), F32), vm((8, 2, 2, 1, 128), F32),
            vm((2 * NX, 2, 2, 1, 128), F32), vm((nz // 2, 2, 2, 1, 128), F32),
            vm((4, 2, 2, 1, 128), F32), vm((2, 8, 128), F32),
            vm((2 * NX, share, snaps), F32), vm((2 * NX, share, snaps), F32),
            vm((nz // 2, share, snaps), F32), vm((2 * NX, share, snaps), F32),
            vm((n, cells), F32), vm((n, snaps), F32),
            dma((9,)), dma((4,)), dma((4,)), dma((2,)), dma((2,)), dma((4,)), dma((4,)),
            dma((4,)), dma((4,)), dma((4,)), dma((4,)), dma((3,)), dma((3,)),
            dma((7,)), dma((7,)), dma((9,)), pltpu.SemaphoreType.REGULAR((4,)),
        ],
        compiler_params=pltpu.CompilerParams(
            collective_id=0, has_side_effects=True, vmem_limit_bytes=52 << 20
        ),
    )(snapshots, jnp.transpose(sketch))
    return deliver(basis, coefficients)


def solution(mesh):
    return jax.shard_map(
        shards,
        mesh=mesh,
        in_specs=(P("cells", "snaps"), P("snaps", None)),
        out_specs=(P(None, "cells"), P(None, "snaps")),
        check_vma=False,
    )
```
